32 devices in a mesh: sect: 4 (over z), dom: 8 (over y, x, core).
Axes of the slice: x: 2, y: 2, z: 4, core: 2. Of those that a mesh axis runs over, the one named last changes fastest.
Arguments:
- state: float32 [2048, 4096], P('sect', 'dom'), may hold values from -6 to 6
- previous: float32 [2048, 4096], P('sect', 'dom'), may hold values from -6 to 6
- coefficient: float32 [2048, 4096], P('sect', 'dom'), may hold values from 0.1 to 0.4
- stiffness: bfloat16 [4, 128, 128], replicated, may hold values from -1 to 1, as said below
- waveform: float32 [8, 32, 512], P(None, ('sect', 'dom')), may hold values from -6 to 6
- entry_face: int32 [1024], P(('sect', 'dom')), may hold values from 0 to 3
- entry_owner: int32 [1024, 1], P(('sect', 'dom')), may hold values from 0 to 7; in each aligned block of 32 rows (0 to 31, 32 to 63, ...) at most 8 rows name the same one
- entry_node: int32 [1024], P(('sect', 'dom')), may hold values from 0 to 3
- rbf: float32 [1024, 128, 128], P(('sect', 'dom')), may hold values from -0.109375 to 0.109375
Outputs:
- state_next: float32 [2048, 4096], P('sect', 'dom')
- previous_next: float32 [2048, 4096], P('sect', 'dom')
- waveform_next: float32 [8, 32, 512], P(None, ('sect', 'dom'))
The draws below stay inside these ranges and needn't reach their ends.
Inputs may be any that keep to these rules, and one draw needn't show every extreme that they name: `entry_owner`: among the entries of one device, at most 8 name the same owner. `stiffness`: each element block is symmetric.
All inputs are finite; a program needn't handle non-finite values.
Results may differ from the reference program's by a relative error of at most 0.0006.
Values sent between devices are 32-bit elements; how exact they have to be, the bound alone decides.
A program may use at most 64 MiB of HBM per device.

```python
import math
import jax
import jax.numpy as jnp
import numpy as np
from jax import lax

ROWS = 512
LANES = 512
SUBSTEPS = 8
BLOCK = 128
ELEM = 128
E_DEV = 32
CAP = 8
BLOCKS = 4
ELEM_BLOCKS = 4
ENTRIES = 1024
FAN = 3072
N_SECT = 4
N_DOM = 8


def draw_stiffness(key, part):
    first_key, second_key = jax.random.split(jax.random.fold_in(key, 17))
    diagonal = jax.random.uniform(first_key, (ELEM_BLOCKS, ELEM), jnp.float32, 0.5, 1.0)
    coupling = jax.random.uniform(second_key, (ELEM_BLOCKS, ELEM, ELEM), jnp.float32, -1.0, 1.0)
    coupling = coupling * (0.6 / ELEM)
    symmetric = 0.5 * (coupling + jnp.swapaxes(coupling, -1, -2))
    identity = jnp.eye(ELEM, dtype=jnp.float32)
    matrix = symmetric * (1.0 - identity) + identity * diagonal[..., None]
    return matrix.astype(jnp.bfloat16)


def place_ends(values, rng, smallest, high):
    longest = values.shape.index(max(values.shape))
    spots = []
    for shift in (0, 1):
        where = [jax.random.randint(jax.random.fold_in(rng, axis), (), 0, length) for axis, length in enumerate(values.shape)]
        where[longest] = (where[longest] + shift) % values.shape[longest]
        spots.append(tuple(where))
    return values.at[spots[0]].set(smallest).at[spots[1]].set(high)


def shard_levels(key, dims, pieces, least, largest):
    def one(dim, parts):
        heights = jax.random.uniform(jax.random.fold_in(jax.random.fold_in(key, 6), dim), (parts,), jnp.float32, least / len(pieces), largest / len(pieces))
        return jnp.repeat(jnp.exp(heights), dims[dim] // parts).reshape((-1,) + (1,) * (len(dims) - dim - 1))

    loudness = one(*pieces[0])
    for cut in pieces[1:]:
        loudness = loudness * one(*cut)
    return loudness


def assign_block(stream_key, own, number, rows, count, top, limit, lean):
    order = jax.random.permutation(stream_key, count)
    packed, usual = load_shares(count, rows * top, limit, lean, True), load_shares(count, rows * top, limit, lean, False)
    places = jnp.arange(count)

    def named(sizes, turn):
        used = int((sizes > 0).sum())
        fixed = max(1, used // 4)
        passed = fixed + (places - fixed + turn * (used - fixed)) % max(1, count - fixed)
        return jnp.zeros((count,), jnp.int32).at[order[jnp.where(places < fixed, places, passed)]].set(jnp.asarray(sizes, jnp.int32))

    sizes = jnp.where(number % 4 == 0, named(packed, number // 4), named(usual, number - number // 4 - 1))
    mixed = jax.random.permutation(jax.random.fold_in(own, 3), count)
    source_of, receiver = mixed[0:count // 2 * 2:2], mixed[1:count // 2 * 2:2]
    room = jnp.minimum(sizes[source_of] - 1, limit - sizes[receiver]) // 2
    room = jnp.where((source_of == order[0]) | (receiver == order[0]) | (sizes[receiver] == 0), 0, jnp.maximum(room, 0))
    passed = jax.random.randint(jax.random.fold_in(own, 4), (count // 2,), 0, 1 << 20) % (room + 1)
    sizes = sizes.at[source_of].add(-passed).at[receiver].add(passed)
    labels = jnp.searchsorted(jnp.cumsum(sizes), jnp.arange(rows * top), side="right").astype(jnp.int32)
    listing = labels.reshape(top, rows).T
    listing = listing[jax.random.permutation(jax.random.fold_in(own, 1), rows)]
    turn = jax.random.randint(jax.random.fold_in(own, 2), (rows, 1), 0, top)
    return jnp.take_along_axis(listing, (jnp.arange(top)[None, :] + turn) % top, axis=1)


def load_shares(amount, total, limit, slope, full):
    weights = [(1 << 20) // math.isqrt(standing ** slope) + 1 for standing in range(1, amount + 1)]
    largest = limit if full else min(limit, max(-(-total // amount), total * weights[0] // sum(weights)))
    least = 1 if total - largest >= amount - 1 else 0
    holding, surplus = [largest] + [least] * (amount - 1), total - largest - least * (amount - 1)
    while surplus > 0:
        candidates = [i for i in range(1, amount) if holding[i] < largest] or [i for i in range(1, amount) if holding[i] < limit]
        pool, remaining = sum([weights[i] for i in candidates]), surplus
        for i in candidates:
            extra = min(limit - holding[i], max(1, remaining * weights[i] // pool), surplus)
            holding[i] = holding[i] + extra
            surplus = surplus - extra
    return np.array(holding)


def gaussian(key, extent, width, reach, cuts=(), kind=jnp.bfloat16):
    level = shard_levels(key, extent, cuts, -0.22, 0.18) if cuts else 1.0
    entries = jax.random.normal(key, extent, jnp.float32) * width * level
    return jnp.minimum(jnp.maximum(entries, -reach), reach).astype(kind)


def setup_inputs(seed: int = 0) -> dict:
    keys = jax.random.split(jax.random.key(seed), 10)
    state = gaussian(keys[0], (N_SECT * ROWS, N_DOM * LANES), 1.0, 6.0, ((0, 4), (1, 8)), jnp.float32)
    previous = gaussian(keys[1], (N_SECT * ROWS, N_DOM * LANES), 1.0, 6.0, ((0, 4), (1, 8)), jnp.float32)
    coefficient = jnp.clip(jnp.exp(math.log(0.4) - 1.3862944 * jax.random.uniform(keys[2], (N_SECT * ROWS, N_DOM * LANES), jnp.float32) ** shard_levels(keys[2], (N_SECT * ROWS, N_DOM * LANES), ((0, 4), (1, 8)), -0.2, 0.2)), 0.1, 0.4)
    stiffness = draw_stiffness(jax.random.fold_in(keys[9], 71), 0)
    waveform = gaussian(keys[4], (SUBSTEPS, N_SECT * N_DOM, LANES), 1.0, 6.0, ((1, 32),), jnp.float32)
    entry_face = place_ends(jax.random.randint(keys[5], (ENTRIES,), 0, BLOCKS), jax.random.fold_in(keys[5], 1), 0, BLOCKS - 1).astype(jnp.int32)
    entry_owner_keys = jax.random.split(jax.random.fold_in(keys[6], 1), ENTRIES // E_DEV)
    entry_owner_turns = jax.random.permutation(jax.random.fold_in(keys[6], 3), ENTRIES // E_DEV)
    entry_owner = jax.vmap(lambda own, number: assign_block(jax.random.fold_in(keys[6], 2), own, number, E_DEV, N_DOM, 1, CAP, 2))(entry_owner_keys, entry_owner_turns).reshape((ENTRIES, 1))
    entry_node = place_ends(jax.random.randint(keys[7], (ENTRIES,), 0, BLOCKS), jax.random.fold_in(keys[7], 1), 0, BLOCKS - 1).astype(jnp.int32)
    rbf = gaussian(keys[8], (ENTRIES, BLOCK, BLOCK), FAN ** -0.5, 0.109375, ((0, 32),), jnp.float32)
    return {"state": state, "previous": previous, "coefficient": coefficient, "stiffness": stiffness, "waveform": waveform, "entry_face": entry_face, "entry_owner": entry_owner, "entry_node": entry_node, "rbf": rbf}


def laplacian(field):
    padded = jnp.pad(field, 1)
    near = padded[:-2, 1:-1] + padded[2:, 1:-1]
    near = near + padded[1:-1, :-2] + padded[1:-1, 2:]
    return near - 4.0 * field


def reference(state, previous, coefficient, stiffness, waveform, entry_face, entry_owner, entry_node, rbf):
    fluid_rows = (N_SECT - 1) * ROWS
    fluid_count = (N_SECT - 1) * N_DOM
    fluid_now, fluid_before = state[:fluid_rows], previous[:fluid_rows]
    shell_now, shell_before = state[fluid_rows:], previous[fluid_rows:]
    fluid_coef, shell_coef = coefficient[:fluid_rows], coefficient[fluid_rows:]
    wet_rows = jnp.arange(N_SECT - 1) * ROWS + ROWS - 1
    matrices = stiffness.astype(jnp.float32)
    face_traces = []
    node_traces = []
    for substep in range(SUBSTEPS):
        fluid_source = jnp.zeros_like(fluid_now).at[wet_rows].set(
            waveform[substep, :fluid_count].reshape(N_SECT - 1, N_DOM * LANES))
        fluid_next = 2.0 * fluid_now - fluid_before + fluid_coef * (laplacian(fluid_now) + fluid_source)
        rounded = lax.optimization_barrier(shell_now.astype(jnp.bfloat16)).astype(jnp.float32)
        element_term = jnp.einsum('bic,bij->bjc', rounded.reshape(ELEM_BLOCKS, ELEM, N_DOM * LANES), matrices,
                                  precision=lax.Precision.HIGHEST).reshape(ROWS, N_DOM * LANES)
        shell_source = jnp.zeros_like(shell_now).at[0].set(waveform[substep, fluid_count:].reshape(N_DOM * LANES))
        shell_next = 2.0 * shell_now - shell_before + shell_coef * (laplacian(shell_now) - element_term + shell_source)
        fluid_before, fluid_now = fluid_now, fluid_next
        shell_before, shell_now = shell_now, shell_next
        face_traces.append(fluid_now[wet_rows].reshape(fluid_count, LANES))
        node_traces.append(shell_now[0].reshape(N_DOM, LANES))
    face_trace = jnp.stack(face_traces)
    node_trace = jnp.stack(node_traces)
    entry_total = fluid_count * E_DEV
    faces = entry_face[:entry_total]
    owners = entry_owner[:entry_total, 0]
    nodes = entry_node[:entry_total]
    weights = rbf[:entry_total]
    device_index = jnp.arange(entry_total, dtype=jnp.int32) // E_DEV
    face_blocks = face_trace.reshape(SUBSTEPS, fluid_count, BLOCKS, BLOCK)
    picked = face_blocks[:, device_index, faces]
    contribution = jnp.einsum('kef,efn->ekn', picked, weights, precision=lax.Precision.HIGHEST)
    node_index = owners * BLOCKS + nodes
    loads = jax.ops.segment_sum(contribution, node_index, N_DOM * BLOCKS)
    loads = loads.reshape(N_DOM, BLOCKS, SUBSTEPS, BLOCK).transpose(2, 0, 1, 3).reshape(SUBSTEPS, N_DOM, LANES)
    node_blocks = node_trace.reshape(SUBSTEPS, N_DOM * BLOCKS, BLOCK)
    fetched = node_blocks[:, node_index]
    face_terms = jnp.einsum('ken,efn->ekf', fetched, weights, precision=lax.Precision.HIGHEST)
    face_index = device_index * BLOCKS + faces
    displacements = jax.ops.segment_sum(face_terms, face_index, fluid_count * BLOCKS)
    displacements = displacements.reshape(fluid_count, BLOCKS, SUBSTEPS, BLOCK).transpose(2, 0, 1, 3).reshape(
        SUBSTEPS, fluid_count, LANES)
    state_next = jnp.concatenate([fluid_now, shell_now], 0)
    previous_next = jnp.concatenate([fluid_before, shell_before], 0)
    waveform_next = jnp.concatenate([displacements, loads], 1)
    return state_next, previous_next, waveform_next
```

```python
import functools

import jax
import jax.numpy as jnp
from jax import lax
from jax.experimental import pallas as pl
from jax.experimental.pallas import tpu as pltpu
from jax.sharding import PartitionSpec as P

HALO = 8
TILE = 128
F32 = jnp.float32
BF16 = jnp.bfloat16


def signal(barrier, section, column):
    pl.semaphore_signal(
        barrier, inc=1, device_id=(section, column), device_id_type=pl.DeviceIdType.MESH
    )


def remote(source, target, send, recv, section, column):
    return pltpu.make_async_remote_copy(
        src_ref=source,
        dst_ref=target,
        send_sem=send,
        recv_sem=recv,
        device_id=(section, column),
        device_id_type=pl.DeviceIdType.MESH,
    )


def halo_kernel(
    n_sect, n_dom, *refs
):
    lefts, rights, tops, bottoms = refs[0:3], refs[3:6], refs[6:9], refs[9:12]
    wave_ref = refs[12]
    sides_ref, wave_out, above_ref, below_ref = refs[13:17]
    (to_left, to_right, from_left, from_right, to_up, to_down, from_up, from_down) = refs[17:25]
    send_sem, recv_sem = refs[25:27]
    s = lax.axis_index("sect")
    d = lax.axis_index("dom")
    rows = sides_ref.shape[1]
    lanes = tops[0].shape[1]
    has_left = d > 0
    has_right = d < n_dom - 1
    has_up = jnp.logical_and(s >= 1, s <= n_sect - 2)
    has_down = s <= n_sect - 3
    places = (
        (has_left, s, d - 1),
        (has_right, s, d + 1),
        (has_up, s - 1, d),
        (has_down, s + 1, d),
    )
    barrier = pltpu.get_barrier_semaphore()
    for has, section, column in places:

        @pl.when(has)
        def _(section=section, column=column):
            signal(barrier, section, column)

    lane = lax.broadcasted_iota(jnp.int32, (rows, TILE), 1)

    def pack(tiles, start):
        a = tiles[0][...]
        b = pltpu.roll(tiles[1][...], (HALO - start) % TILE, 1)
        c = pltpu.roll(tiles[2][...], (2 * HALO - start) % TILE, 1)
        if start:
            a = pltpu.roll(a, TILE - start, 1)
        packed = jnp.where(lane < HALO, a, jnp.where(lane < 2 * HALO, b, c))
        return packed.T[: 3 * HALO]

    to_left[: 3 * HALO] = pack(lefts, 0)
    to_left[3 * HALO :, :TILE] = wave_ref[:, :TILE]
    to_left[3 * HALO :, TILE:] = jnp.zeros((HALO, rows - TILE), F32)
    to_right[: 3 * HALO] = pack(rights, TILE - HALO)
    to_right[3 * HALO :, :TILE] = wave_ref[:, lanes - TILE :]
    to_right[3 * HALO :, TILE:] = jnp.zeros((HALO, rows - TILE), F32)

    peers = sum(jnp.where(has, 1, 0).astype(jnp.int32) for has, _, _ in places)
    pl.semaphore_wait(barrier, peers)

    go_left = remote(to_left, from_right, send_sem.at[0], recv_sem.at[0], s, d - 1)
    go_right = remote(to_right, from_left, send_sem.at[1], recv_sem.at[1], s, d + 1)

    @pl.when(has_left)
    def _():
        go_left.start()

    @pl.when(has_right)
    def _():
        go_right.start()

    @pl.when(has_right)
    def _():
        go_left.wait_recv()

    @pl.when(jnp.logical_not(has_right))
    def _():
        from_right[...] = jnp.zeros_like(from_right)

    @pl.when(has_left)
    def _():
        go_right.wait_recv()

    @pl.when(jnp.logical_not(has_left))
    def _():
        from_left[...] = jnp.zeros_like(from_left)

    fill = jnp.zeros((TILE - 3 * HALO, rows), F32)
    right = jnp.concatenate([from_right[: 3 * HALO], fill], 0).T
    left = jnp.concatenate([from_left[: 3 * HALO], fill], 0).T
    for a in range(3):
        r = pltpu.roll(right, (TILE - a * HALO) % TILE, 1) if a else right
        le = pltpu.roll(left, TILE - (a + 1) * HALO, 1)
        sides_ref[a] = jnp.where(lane < HALO, r, jnp.where(lane >= TILE - HALO, le, 0.0))
        part = pl.ds(a * HALO, HALO)
        to_up[part, :lanes] = tops[a][...]
        to_up[part, lanes:] = sides_ref[a, :HALO]
        to_down[part, :lanes] = bottoms[a][...]
        to_down[part, lanes:] = sides_ref[a, rows - HALO :]
    lane8 = lane[:HALO]
    wave_side = jnp.where(
        lane8 < HALO,
        from_right[3 * HALO :, :TILE],
        jnp.where(lane8 >= TILE - HALO, from_left[3 * HALO :, :TILE], 0.0),
    )
    wave_out[:, :lanes] = wave_ref[...]
    wave_out[:, lanes:] = wave_side
    to_down[3 * HALO :, :lanes] = wave_ref[...]
    to_down[3 * HALO :, lanes:] = wave_side

    go_up = remote(to_up, from_down, send_sem.at[2], recv_sem.at[2], s - 1, d)
    go_down = remote(to_down, from_up, send_sem.at[3], recv_sem.at[3], s + 1, d)

    @pl.when(has_up)
    def _():
        go_up.start()

    @pl.when(has_down)
    def _():
        go_down.start()

    @pl.when(has_down)
    def _():
        go_up.wait_recv()
        below_ref[...] = from_down[...]

    @pl.when(jnp.logical_not(has_down))
    def _():
        below_ref[...] = jnp.zeros_like(below_ref)

    @pl.when(has_up)
    def _():
        go_down.wait_recv()
        above_ref[...] = from_up[...]

    @pl.when(jnp.logical_not(has_up))
    def _():
        above_ref[...] = jnp.zeros_like(above_ref)

    for has, copy in (
        (has_left, go_left),
        (has_right, go_right),
        (has_up, go_up),
        (has_down, go_down),
    ):

        @pl.when(has)
        def _(copy=copy):
            copy.wait_send()


def exchange(state, previous, coefficient, wave, n_sect, n_dom):
    rows, lanes = state.shape
    fields = (state, previous, coefficient)
    last = lanes // TILE - 1
    wide = lanes + TILE

    def spec(shape, where):
        return pl.BlockSpec(shape, lambda i: where)

    return pl.pallas_call(
        functools.partial(halo_kernel, n_sect, n_dom),
        grid=(1,),
        out_shape=(
            jax.ShapeDtypeStruct((3, rows, TILE), F32),
            jax.ShapeDtypeStruct((HALO, wide), F32),
            jax.ShapeDtypeStruct((4 * HALO, wide), F32),
            jax.ShapeDtypeStruct((3 * HALO, wide), F32),
        ),
        in_specs=[spec((rows, TILE), (0, 0))] * 3
        + [spec((rows, TILE), (0, last))] * 3
        + [spec((HALO, lanes), (0, 0))] * 3
        + [spec((HALO, lanes), (rows // HALO - 1, 0))] * 3
        + [spec((HALO, lanes), (0, 0))],
        out_specs=(
            pl.BlockSpec((3, rows, TILE), lambda i: (0, 0, 0)),
            spec((HALO, wide), (0, 0)),
            spec((4 * HALO, wide), (0, 0)),
            spec((3 * HALO, wide), (0, 0)),
        ),
        scratch_shapes=[pltpu.VMEM((4 * HALO, rows), F32)] * 4
        + [
            pltpu.VMEM((3 * HALO, wide), F32),
            pltpu.VMEM((4 * HALO, wide), F32),
            pltpu.VMEM((4 * HALO, wide), F32),
            pltpu.VMEM((3 * HALO, wide), F32),
            pltpu.SemaphoreType.DMA((4,)),
            pltpu.SemaphoreType.DMA((4,)),
        ],
        compiler_params=pltpu.CompilerParams(collective_id=0, has_side_effects=True),
        name="halo",
    )(*fields, *fields, *fields, *fields, wave)


CHUNK = 24


def window_kernel(
    n_sect, state, previous, coefficient, stiffness, sides, wave, above, below,
    state_out, previous_out, trace_out, first, second, coef,
):
    rows, lanes = state.shape
    wide = lanes + TILE
    full = rows + 2 * HALO
    s = lax.axis_index("sect")
    on_shell = s == n_sect - 1
    for a, (ref, center) in enumerate(((first, state), (second, previous), (coef, coefficient))):
        part = pl.ds(a * HALO, HALO)
        ref[:HALO] = above[part]
        ref[HALO + rows :] = below[part]
        ref[HALO : HALO + rows, :lanes] = center[...]
        ref[HALO : HALO + rows, lanes:] = sides[a]
    substeps = wave.shape[0]
    shell_scale = jnp.where(on_shell, 1.0, 0.0).astype(F32)
    fluid_scale = 1.0 - shell_scale
    elem_blocks, elem = stiffness.shape[0], stiffness.shape[1]

    def step(k, cur, other):
        for start in range(0, full, CHUNK):
            stop = min(start + CHUNK, full)
            here = cur[start:stop, :]
            if start == 0:
                up = pltpu.roll(here, 1, 0)
            else:
                up = cur[start - 1 : stop - 1, :]
            if stop == full:
                down = pltpu.roll(here, stop - start - 1, 0)
            else:
                down = cur[start + 1 : stop + 1, :]
            near = (up + down) + pltpu.roll(here, 1, 1) + pltpu.roll(here, wide - 1, 1)
            other[start:stop, :] = (
                2.0 * here - other[start:stop, :] + coef[start:stop, :] * (near - 4.0 * here)
            )
        row = wave[pl.ds(k, 1), :]
        up_row = above[pl.ds(3 * HALO + k, 1), :]
        other[HALO - 1 : HALO, :] += coef[HALO - 1 : HALO, :] * (up_row * fluid_scale)
        other[HALO : HALO + 1, :] += coef[HALO : HALO + 1, :] * (row * shell_scale)
        at = HALO + rows - 1
        other[at : at + 1, :] += coef[at : at + 1, :] * (row * fluid_scale)

        @pl.when(on_shell)
        def _():
            for b in range(elem_blocks):
                part = slice(HALO + b * elem, HALO + (b + 1) * elem)
                term = jnp.dot(
                    stiffness[b], cur[part, :].astype(BF16), preferred_element_type=F32
                )
                other[part, :] -= coef[part, :] * term

        seen = jnp.where(
            on_shell, other[HALO : HALO + 1, :lanes], other[at : at + 1, :lanes]
        )
        for b in range(lanes // TILE):
            trace_out[b, pl.ds(k, 1), :] = seen[:, b * TILE : (b + 1) * TILE]

    def pair(i, carry):
        step(2 * i, first, second)
        step(2 * i + 1, second, first)
        return carry

    lax.fori_loop(0, substeps // 2, pair, 0)
    state_out[...] = first[HALO : HALO + rows, :lanes]
    previous_out[...] = second[HALO : HALO + rows, :lanes]


def window(state, previous, coefficient, stiffness, sides, wave, above, below, n_sect):
    rows, lanes = state.shape
    substeps = wave.shape[0]
    return pl.pallas_call(
        functools.partial(window_kernel, n_sect),
        out_shape=(
            jax.ShapeDtypeStruct((rows, lanes), F32),
            jax.ShapeDtypeStruct((rows, lanes), F32),
            jax.ShapeDtypeStruct((lanes // TILE, substeps, TILE), F32),
        ),
        in_specs=[pl.BlockSpec(memory_space=pltpu.VMEM)] * 8,
        out_specs=(pl.BlockSpec(memory_space=pltpu.VMEM),) * 3,
        scratch_shapes=[pltpu.VMEM((rows + 2 * HALO, lanes + TILE), F32)] * 3,
        compiler_params=pltpu.CompilerParams(vmem_limit_bytes=40 * 1024 * 1024),
        name="window",
    )(state, previous, coefficient, stiffness, sides, wave, above, below)


def split(value):
    high = value.astype(BF16)
    low = (value - high.astype(F32)).astype(BF16)
    return high, low


def three_products(x, w, contract):
    x_high, x_low = split(x)
    w_high, w_low = split(w)
    dims = (((1,), (contract,)), ((), ()))
    out = lax.dot_general(x_high, w_high, dims, preferred_element_type=F32)
    out += lax.dot_general(x_low, w_high, dims, preferred_element_type=F32)
    out += lax.dot_general(x_high, w_low, dims, preferred_element_type=F32)
    return out


def push_kernel(n_sect, face, owner, node, trace, rbf, out, terms):
    entries = rbf.shape[0]
    blocks = trace.shape[0]

    @pl.when(lax.axis_index("sect") < n_sect - 1)
    def _():
        out[...] = jnp.zeros_like(out)
        for e in range(entries):
            terms[e] = three_products(trace[face[e]], rbf[e], 0)
        for e in range(entries):
            slot = owner[e] * blocks + node[e]
            out[slot] += terms[e]


def push(face, owner, node, trace, rbf, n_sect, n_dom):
    blocks, substeps, size = trace.shape
    return pl.pallas_call(
        functools.partial(push_kernel, n_sect),
        out_shape=jax.ShapeDtypeStruct((n_dom * blocks, substeps, size), F32),
        in_specs=[pl.BlockSpec(memory_space=pltpu.SMEM)] * 3
        + [pl.BlockSpec(memory_space=pltpu.VMEM)] * 2,
        out_specs=pl.BlockSpec(memory_space=pltpu.VMEM),
        scratch_shapes=[pltpu.VMEM((rbf.shape[0], substeps, size), F32)],
        name="push",
    )(face, owner, node, trace, rbf)


def swap_kernel(
    n_sect, n_dom, outgoing, trace, loads_out, nodes_out,
    arrived, total, parts, nodes, shell_trace,
    load_send, load_recv, part_send, part_recv, down_send, down_recv, node_send, node_recv,
):
    s = lax.axis_index("sect")
    d = lax.axis_index("dom")
    blocks = trace.shape[0]
    shell = n_sect - 1
    on_shell = s == shell
    barrier = pltpu.get_barrier_semaphore()

    @pl.when(on_shell)
    def _():
        for t in range(shell):
            signal(barrier, t, d)
        pl.semaphore_wait(barrier, shell)

    @pl.when(jnp.logical_not(on_shell))
    def _():
        for j in range(1, n_dom):
            signal(barrier, s, lax.rem(d + j, n_dom))
        signal(barrier, shell, d)
        pl.semaphore_wait(barrier, n_dom)

    @pl.when(on_shell)
    def _():
        copies = []
        for t in range(shell):
            copy = remote(trace, shell_trace, down_send.at[t], down_recv, t, d)
            copy.start()
            copies.append(copy)
        nodes_out[...] = jnp.zeros_like(nodes_out)
        for t in range(shell):
            remote(total, parts.at[t], part_send, part_recv.at[t], t, d).wait_recv()
        loads = parts[0]
        for t in range(1, shell):
            loads = loads + parts[t]
        loads_out[...] = loads
        for copy in copies:
            copy.wait_send()

    @pl.when(jnp.logical_not(on_shell))
    def _():
        loads = []
        for j in range(1, n_dom):
            to = lax.rem(d + j, n_dom)
            copy = remote(
                outgoing.at[pl.ds(to * blocks, blocks)], arrived.at[j - 1],
                load_send.at[j - 1], load_recv.at[j - 1], s, to,
            )
            copy.start()
            loads.append(copy)
        value = outgoing[pl.ds(d * blocks, blocks)]
        for j in range(1, n_dom):
            loads[j - 1].wait_recv()
            value = value + arrived[j - 1]
        total[...] = value
        up = remote(total, parts.at[s], part_send, part_recv.at[s], shell, d)
        up.start()
        remote(trace, shell_trace, down_send.at[0], down_recv, shell, d).wait_recv()
        sends = []
        for j in range(1, n_dom):
            to = lax.rem(d + j, n_dom)
            copy = remote(
                shell_trace, nodes.at[j - 1], node_send.at[j - 1], node_recv.at[j - 1], s, to
            )
            copy.start()
            sends.append(copy)
        loads_out[...] = jnp.zeros_like(loads_out)
        nodes_out[0] = shell_trace[...]
        for j in range(1, n_dom):
            sends[j - 1].wait_recv()
            nodes_out[j] = nodes[j - 1]
        for copy in loads + sends + [up]:
            copy.wait_send()


def swap(outgoing, trace, n_sect, n_dom):
    block = trace.shape
    dma = pltpu.SemaphoreType.DMA
    return pl.pallas_call(
        functools.partial(swap_kernel, n_sect, n_dom),
        out_shape=(
            jax.ShapeDtypeStruct(block, F32),
            jax.ShapeDtypeStruct((n_dom,) + block, F32),
        ),
        in_specs=[pl.BlockSpec(memory_space=pltpu.VMEM)] * 2,
        out_specs=(pl.BlockSpec(memory_space=pltpu.VMEM),) * 2,
        scratch_shapes=[
            pltpu.VMEM((n_dom - 1,) + block, F32),
            pltpu.VMEM(block, F32),
            pltpu.VMEM((n_sect - 1,) + block, F32),
            pltpu.VMEM((n_dom - 1,) + block, F32),
            pltpu.VMEM(block, F32),
            dma((n_dom - 1,)),
            dma((n_dom - 1,)),
            dma,
            dma((n_sect - 1,)),
            dma((n_sect - 1,)),
            dma,
            dma((n_dom - 1,)),
            dma((n_dom - 1,)),
        ],
        compiler_params=pltpu.CompilerParams(collective_id=1, has_side_effects=True),
        name="swap",
    )(outgoing, trace)


def pull_kernel(n_sect, n_dom, face, owner, node, loads, nodes, rbf, out, terms, sums):
    entries = rbf.shape[0]
    blocks = loads.shape[0]
    d = lax.axis_index("dom")
    on_shell = lax.axis_index("sect") == n_sect - 1

    @pl.when(on_shell)
    def _():
        for b in range(blocks):
            out[:, b * TILE : (b + 1) * TILE] = loads[b]

    @pl.when(jnp.logical_not(on_shell))
    def _():
        sums[...] = jnp.zeros_like(sums)
        for e in range(entries):
            slot = lax.rem(d - owner[e] + n_dom, n_dom)
            terms[e] = three_products(nodes[slot, node[e]], rbf[e], 1)
        for e in range(entries):
            sums[face[e]] += terms[e]
        for b in range(blocks):
            out[:, b * TILE : (b + 1) * TILE] = sums[b]


def pull(face, owner, node, loads, nodes, rbf, n_sect, n_dom):
    blocks, substeps, size = loads.shape
    return pl.pallas_call(
        functools.partial(pull_kernel, n_sect, n_dom),
        out_shape=jax.ShapeDtypeStruct((substeps, blocks * size), F32),
        in_specs=[pl.BlockSpec(memory_space=pltpu.SMEM)] * 3
        + [pl.BlockSpec(memory_space=pltpu.VMEM)] * 3,
        out_specs=pl.BlockSpec(memory_space=pltpu.VMEM),
        scratch_shapes=[
            pltpu.VMEM((rbf.shape[0], substeps, size), F32),
            pltpu.VMEM((blocks, substeps, size), F32),
        ],
        name="pull",
    )(face, owner, node, loads, nodes, rbf)


def local(
    state, previous, coefficient, stiffness, waveform, entry_face, entry_owner, entry_node, rbf
):
    n_sect = lax.axis_size("sect")
    n_dom = lax.axis_size("dom")
    owner = entry_owner[:, 0]
    wave = waveform[:, 0, :]
    sides, wide_wave, above, below = exchange(state, previous, coefficient, wave, n_sect, n_dom)
    current, before, trace = window(
        state, previous, coefficient, stiffness, sides, wide_wave, above, below, n_sect
    )
    outgoing = push(entry_face, owner, entry_node, trace, rbf, n_sect, n_dom)
    loads, nodes = swap(outgoing, trace, n_sect, n_dom)
    out = pull(entry_face, owner, entry_node, loads, nodes, rbf, n_sect, n_dom)
    return (current, before, out[:, None, :])


def solution(mesh):
    in_specs = (
        P("sect", "dom"),
        P("sect", "dom"),
        P("sect", "dom"),
        P(),
        P(None, ("sect", "dom"), None),
        P(("sect", "dom")),
        P(("sect", "dom"), None),
        P(("sect", "dom")),
        P(("sect", "dom"), None, None),
    )
    out_specs = (P("sect", "dom"), P("sect", "dom"), P(None, ("sect", "dom"), None))
    return jax.shard_map(local, mesh=mesh, in_specs=in_specs, out_specs=out_specs, check_vma=False)
```

```python
import functools

import jax
import jax.numpy as jnp
from jax import lax
from jax.experimental import pallas as pl
from jax.experimental.pallas import tpu as pltpu
from jax.sharding import PartitionSpec as P

HALO = 8
TILE = 128
F32 = jnp.float32
BF16 = jnp.bfloat16


def signal(barrier, section, column):
    pl.semaphore_signal(
        barrier, inc=1, device_id=(section, column), device_id_type=pl.DeviceIdType.MESH
    )


def remote(source, target, send, recv, section, column):
    return pltpu.make_async_remote_copy(
        src_ref=source,
        dst_ref=target,
        send_sem=send,
        recv_sem=recv,
        device_id=(section, column),
        device_id_type=pl.DeviceIdType.MESH,
    )


def halo_kernel(n_sect, n_dom, *refs):
    fields = refs[0:3]
    wave_ref = refs[3]
    sides_ref, wave_out, above_ref, below_ref = refs[4:8]
    to_left, to_right, from_left, from_right, to_up, to_down, from_up, from_down = refs[8:16]
    from_up_left, from_up_right, from_down_left, from_down_right = refs[16:20]
    send_sem, recv_sem = refs[20:22]
    s = lax.axis_index("sect")
    d = lax.axis_index("dom")
    rows, lanes = fields[0].shape
    substeps = wave_ref.shape[0]
    has_left = d > 0
    has_right = d < n_dom - 1
    has_up = jnp.logical_and(s >= 1, s <= n_sect - 2)
    has_down = s <= n_sect - 3
    both = jnp.logical_and
    first = pl.ds(0, TILE)
    last = pl.ds(lanes - TILE, TILE)
    routes = (
        (has_up, s - 1, d, to_up, from_down, has_down, from_down),
        (has_down, s + 1, d, to_down, from_up, has_up, from_up),
        (has_left, s, d - 1, to_left, from_right, has_right, from_right),
        (has_right, s, d + 1, to_right, from_left, has_left, from_left),
        (both(has_up, has_left), s - 1, d - 1, to_up.at[:, first], from_down_right,
         both(has_down, has_right), from_down_right),
        (both(has_up, has_right), s - 1, d + 1, to_up.at[:, last], from_down_left,
         both(has_down, has_left), from_down_left),
        (both(has_down, has_left), s + 1, d - 1, to_down.at[:, first], from_up_right,
         both(has_up, has_right), from_up_right),
        (both(has_down, has_right), s + 1, d + 1, to_down.at[:, last], from_up_left,
         both(has_up, has_left), from_up_left),
    )
    barrier = pltpu.get_barrier_semaphore()
    for has, section, column, *_ in routes:

        @pl.when(has)
        def _(section=section, column=column):
            signal(barrier, section, column)

    wave = jnp.concatenate([wave_ref[k] for k in range(substeps)], 0)
    for a in range(3):
        part = pl.ds(a * HALO, HALO)
        to_up[part] = fields[a][:HALO]
        to_down[part] = fields[a][rows - HALO :]
    to_down[3 * HALO :] = wave
    lane = lax.broadcasted_iota(jnp.int32, (rows, TILE), 1)

    def pack(where, start):
        a = fields[0][:, where]
        b = pltpu.roll(fields[1][:, where], (HALO - start) % TILE, 1)
        c = pltpu.roll(fields[2][:, where], (2 * HALO - start) % TILE, 1)
        if start:
            a = pltpu.roll(a, TILE - start, 1)
        packed = jnp.where(lane < HALO, a, jnp.where(lane < 2 * HALO, b, c))
        return packed.T[: 3 * HALO]

    to_left[: 3 * HALO] = pack(first, 0)
    to_left[3 * HALO :, :TILE] = wave[:, :TILE]
    to_left[3 * HALO :, TILE:] = jnp.zeros((HALO, rows - TILE), F32)
    to_right[: 3 * HALO] = pack(last, TILE - HALO)
    to_right[3 * HALO :, :TILE] = wave[:, lanes - TILE :]
    to_right[3 * HALO :, TILE:] = jnp.zeros((HALO, rows - TILE), F32)

    peers = sum(jnp.where(route[0], 1, 0).astype(jnp.int32) for route in routes)
    pl.semaphore_wait(barrier, peers)

    copies = []
    for i, (has, section, column, source, target, _, _) in enumerate(routes):
        copy = remote(source, target, send_sem.at[i], recv_sem.at[i], section, column)
        copies.append(copy)

        @pl.when(has)
        def _(copy=copy):
            copy.start()

    wave_out[:, :lanes] = wave
    for i in (2, 3, 0, 1, 4, 5, 6, 7):
        comes, buf = routes[i][5:]

        @pl.when(comes)
        def _(copy=copies[i]):
            copy.wait_recv()

        @pl.when(jnp.logical_not(comes))
        def _(buf=buf):
            buf[...] = jnp.zeros_like(buf)

        if i == 3:
            fill = jnp.zeros((TILE - 3 * HALO, rows), F32)
            right = jnp.concatenate([from_right[: 3 * HALO], fill], 0).T
            left = jnp.concatenate([from_left[: 3 * HALO], fill], 0).T
            for a in range(3):
                r = pltpu.roll(right, (TILE - a * HALO) % TILE, 1) if a else right
                le = pltpu.roll(left, TILE - (a + 1) * HALO, 1)
                sides_ref[a] = jnp.where(
                    lane < HALO, r, jnp.where(lane >= TILE - HALO, le, 0.0)
                )

    def join(right_part, left_part):
        at = lax.broadcasted_iota(jnp.int32, right_part.shape, 1)
        return jnp.where(at < HALO, right_part, jnp.where(at >= TILE - HALO, left_part, 0.0))

    wave_out[:, lanes:] = join(from_right[3 * HALO :, :TILE], from_left[3 * HALO :, :TILE])
    above_ref[:, :lanes] = from_up[...]
    above_ref[:, lanes:] = join(from_up_right[...], from_up_left[...])
    below_ref[:, :lanes] = from_down[...]
    below_ref[:, lanes:] = join(from_down_right[...], from_down_left[...])

    for route, copy in zip(routes, copies):

        @pl.when(route[0])
        def _(copy=copy):
            copy.wait_send()


def exchange(state, previous, coefficient, wave, n_sect, n_dom):
    rows, lanes = state.shape
    wide = lanes + TILE
    vmem = pl.BlockSpec(memory_space=pltpu.VMEM)
    return pl.pallas_call(
        functools.partial(halo_kernel, n_sect, n_dom),
        out_shape=(
            jax.ShapeDtypeStruct((3, rows, TILE), F32),
            jax.ShapeDtypeStruct((HALO, wide), F32),
            jax.ShapeDtypeStruct((4 * HALO, wide), F32),
            jax.ShapeDtypeStruct((3 * HALO, wide), F32),
        ),
        in_specs=[vmem] * 4,
        out_specs=(vmem,) * 4,
        scratch_shapes=[pltpu.VMEM((4 * HALO, rows), F32)] * 4
        + [
            pltpu.VMEM((3 * HALO, lanes), F32),
            pltpu.VMEM((4 * HALO, lanes), F32),
            pltpu.VMEM((4 * HALO, lanes), F32),
            pltpu.VMEM((3 * HALO, lanes), F32),
            pltpu.VMEM((4 * HALO, TILE), F32),
            pltpu.VMEM((4 * HALO, TILE), F32),
            pltpu.VMEM((3 * HALO, TILE), F32),
            pltpu.VMEM((3 * HALO, TILE), F32),
            pltpu.SemaphoreType.DMA((8,)),
            pltpu.SemaphoreType.DMA((8,)),
        ],
        compiler_params=pltpu.CompilerParams(collective_id=0, has_side_effects=True),
        name="halo",
    )(state, previous, coefficient, wave)


CHUNK = 24


def window_kernel(
    n_sect, face, owner, node, state, previous, coefficient, stiffness, sides, wave, above,
    below, rbf, state_out, previous_out, trace_out, slots, high, low, first, second, coef, terms,
):
    rows, lanes = state.shape
    wide = lanes + TILE
    full = rows + 2 * HALO
    s = lax.axis_index("sect")
    on_shell = s == n_sect - 1
    for a, (ref, center) in enumerate(((first, state), (second, previous), (coef, coefficient))):
        part = pl.ds(a * HALO, HALO)
        ref[:HALO] = above[part]
        ref[HALO + rows :] = below[part]
        ref[HALO : HALO + rows, :lanes] = center[...]
        ref[HALO : HALO + rows, lanes:] = sides[a]
    substeps = wave.shape[0]
    shell_scale = jnp.where(on_shell, 1.0, 0.0).astype(F32)
    fluid_scale = 1.0 - shell_scale
    elem_blocks, elem = stiffness.shape[0], stiffness.shape[1]

    def step(k, cur, other):
        for start in range(0, full, CHUNK):
            stop = min(start + CHUNK, full)
            here = cur[start:stop, :]
            if start == 0:
                up = pltpu.roll(here, 1, 0)
            else:
                up = cur[start - 1 : stop - 1, :]
            if stop == full:
                down = pltpu.roll(here, stop - start - 1, 0)
            else:
                down = cur[start + 1 : stop + 1, :]
            near = (up + down) + pltpu.roll(here, 1, 1) + pltpu.roll(here, wide - 1, 1)
            other[start:stop, :] = (
                2.0 * here - other[start:stop, :] + coef[start:stop, :] * (near - 4.0 * here)
            )
        row = wave[pl.ds(k, 1), :]
        up_row = above[pl.ds(3 * HALO + k, 1), :]
        other[HALO - 1 : HALO, :] += coef[HALO - 1 : HALO, :] * (up_row * fluid_scale)
        other[HALO : HALO + 1, :] += coef[HALO : HALO + 1, :] * (row * shell_scale)
        at = HALO + rows - 1
        other[at : at + 1, :] += coef[at : at + 1, :] * (row * fluid_scale)

        @pl.when(on_shell)
        def _():
            for b in range(elem_blocks):
                part = slice(HALO + b * elem, HALO + (b + 1) * elem)
                term = jnp.dot(
                    stiffness[b], cur[part, :].astype(BF16), preferred_element_type=F32
                )
                other[part, :] -= coef[part, :] * term

        seen = jnp.where(
            on_shell, other[HALO : HALO + 1, :lanes], other[at : at + 1, :lanes]
        )
        for b in range(lanes // TILE):
            trace_out[b, pl.ds(k, 1), :] = seen[:, b * TILE : (b + 1) * TILE]

    def pair(i, carry):
        step(2 * i, first, second)
        step(2 * i + 1, second, first)
        return carry

    lax.fori_loop(0, substeps // 2, pair, 0)
    state_out[...] = first[HALO : HALO + rows, :lanes]
    previous_out[...] = second[HALO : HALO + rows, :lanes]


    entries = rbf.shape[0]
    blocks = trace_out.shape[0]

    @pl.when(jnp.logical_not(on_shell))
    def _():
        slots[...] = jnp.zeros_like(slots)
        for e in range(entries):
            w_high, w_low = split(rbf[e])
            high[e] = w_high
            low[e] = w_low
            terms[e] = three_products(trace_out[face[e]], w_high, w_low, 0)
        for e in range(entries):
            slots[owner[e, 0] * blocks + node[e]] += terms[e]


def window(
    face, owner, node, state, previous, coefficient, stiffness, sides, wave, above, below, rbf,
    n_sect, n_dom,
):
    rows, lanes = state.shape
    substeps = wave.shape[0]
    blocks = lanes // TILE
    vmem = pl.BlockSpec(memory_space=pltpu.VMEM)
    return pl.pallas_call(
        functools.partial(window_kernel, n_sect),
        out_shape=(
            jax.ShapeDtypeStruct((rows, lanes), F32),
            jax.ShapeDtypeStruct((rows, lanes), F32),
            jax.ShapeDtypeStruct((blocks, substeps, TILE), F32),
            jax.ShapeDtypeStruct((n_dom * blocks, substeps, TILE), F32),
            jax.ShapeDtypeStruct(rbf.shape, BF16),
            jax.ShapeDtypeStruct(rbf.shape, BF16),
        ),
        in_specs=[pl.BlockSpec(memory_space=pltpu.SMEM)] * 3 + [vmem] * 9,
        out_specs=(vmem,) * 6,
        scratch_shapes=[pltpu.VMEM((rows + 2 * HALO, lanes + TILE), F32)] * 3
        + [pltpu.VMEM((rbf.shape[0], substeps, TILE), F32)],
        compiler_params=pltpu.CompilerParams(vmem_limit_bytes=40 * 1024 * 1024),
        name="window",
    )(
        face, owner, node, state, previous, coefficient, stiffness, sides, wave, above, below,
        rbf,
    )


def split(value):
    high = value.astype(BF16)
    low = (value - high.astype(F32)).astype(BF16)
    return high, low


def three_products(x, w_high, w_low, contract):
    x_high, x_low = split(x)
    dims = (((1,), (contract,)), ((), ()))
    out = lax.dot_general(x_high, w_high, dims, preferred_element_type=F32)
    out += lax.dot_general(x_low, w_high, dims, preferred_element_type=F32)
    out += lax.dot_general(x_high, w_low, dims, preferred_element_type=F32)
    return out


def swap_kernel(
    n_sect, n_dom, outgoing, trace, loads_out, nodes_out,
    arrived, total, parts, nodes, shell_trace,
    load_send, load_recv, part_send, part_recv, down_send, down_recv, node_send, node_recv,
):
    s = lax.axis_index("sect")
    d = lax.axis_index("dom")
    blocks = trace.shape[0]
    shell = n_sect - 1
    on_shell = s == shell
    barrier = pltpu.get_barrier_semaphore()

    @pl.when(on_shell)
    def _():
        for t in range(shell):
            signal(barrier, t, d)
        pl.semaphore_wait(barrier, shell)

    @pl.when(jnp.logical_not(on_shell))
    def _():
        for j in range(1, n_dom):
            signal(barrier, s, lax.rem(d + j, n_dom))
        signal(barrier, shell, d)
        pl.semaphore_wait(barrier, n_dom)

    @pl.when(on_shell)
    def _():
        copies = []
        for t in range(shell):
            copy = remote(trace, shell_trace, down_send.at[t], down_recv, t, d)
            copy.start()
            copies.append(copy)
        nodes_out[...] = jnp.zeros_like(nodes_out)
        for t in range(shell):
            remote(total, parts.at[t], part_send, part_recv.at[t], t, d).wait_recv()
        loads = parts[0]
        for t in range(1, shell):
            loads = loads + parts[t]
        loads_out[...] = loads
        for copy in copies:
            copy.wait_send()

    @pl.when(jnp.logical_not(on_shell))
    def _():
        loads = []
        for j in range(1, n_dom):
            to = lax.rem(d + j, n_dom)
            copy = remote(
                outgoing.at[pl.ds(to * blocks, blocks)], arrived.at[j - 1],
                load_send.at[j - 1], load_recv.at[j - 1], s, to,
            )
            copy.start()
            loads.append(copy)
        remote(trace, shell_trace, down_send.at[0], down_recv, shell, d).wait_recv()
        sends = []
        for j in range(1, n_dom):
            to = lax.rem(d + j, n_dom)
            copy = remote(
                shell_trace, nodes.at[j - 1], node_send.at[j - 1], node_recv.at[j - 1], s, to
            )
            copy.start()
            sends.append(copy)
        value = outgoing[pl.ds(d * blocks, blocks)]
        for j in range(1, n_dom):
            loads[j - 1].wait_recv()
            value = value + arrived[j - 1]
        total[...] = value
        up = remote(total, parts.at[s], part_send, part_recv.at[s], shell, d)
        up.start()
        loads_out[...] = jnp.zeros_like(loads_out)
        nodes_out[0] = shell_trace[...]
        for j in range(1, n_dom):
            sends[j - 1].wait_recv()
            nodes_out[j] = nodes[j - 1]
        for copy in loads + sends + [up]:
            copy.wait_send()


def swap(outgoing, trace, n_sect, n_dom):
    block = trace.shape
    dma = pltpu.SemaphoreType.DMA
    return pl.pallas_call(
        functools.partial(swap_kernel, n_sect, n_dom),
        out_shape=(
            jax.ShapeDtypeStruct(block, F32),
            jax.ShapeDtypeStruct((n_dom,) + block, F32),
        ),
        in_specs=[pl.BlockSpec(memory_space=pltpu.VMEM)] * 2,
        out_specs=(pl.BlockSpec(memory_space=pltpu.VMEM),) * 2,
        scratch_shapes=[
            pltpu.VMEM((n_dom - 1,) + block, F32),
            pltpu.VMEM(block, F32),
            pltpu.VMEM((n_sect - 1,) + block, F32),
            pltpu.VMEM((n_dom - 1,) + block, F32),
            pltpu.VMEM(block, F32),
            dma((n_dom - 1,)),
            dma((n_dom - 1,)),
            dma,
            dma((n_sect - 1,)),
            dma((n_sect - 1,)),
            dma,
            dma((n_dom - 1,)),
            dma((n_dom - 1,)),
        ],
        compiler_params=pltpu.CompilerParams(collective_id=1, has_side_effects=True),
        name="swap",
    )(outgoing, trace)


def pull_kernel(n_sect, n_dom, face, owner, node, loads, nodes, high, low, out, terms, sums):
    entries = high.shape[0]
    substeps = out.shape[0]
    blocks = loads.shape[0]
    d = lax.axis_index("dom")
    on_shell = lax.axis_index("sect") == n_sect - 1

    @pl.when(on_shell)
    def _():
        for b in range(blocks):
            for k in range(substeps):
                out[k, :, b * TILE : (b + 1) * TILE] = loads[b, k : k + 1, :]

    @pl.when(jnp.logical_not(on_shell))
    def _():
        sums[...] = jnp.zeros_like(sums)
        for e in range(entries):
            slot = lax.rem(d - owner[e, 0] + n_dom, n_dom)
            terms[e] = three_products(nodes[slot, node[e]], high[e], low[e], 1)
        for e in range(entries):
            sums[face[e]] += terms[e]
        for b in range(blocks):
            for k in range(substeps):
                out[k, :, b * TILE : (b + 1) * TILE] = sums[b, k : k + 1, :]


def pull(face, owner, node, loads, nodes, high, low, n_sect, n_dom):
    blocks, substeps, size = loads.shape
    return pl.pallas_call(
        functools.partial(pull_kernel, n_sect, n_dom),
        out_shape=jax.ShapeDtypeStruct((substeps, 1, blocks * size), F32),
        in_specs=[pl.BlockSpec(memory_space=pltpu.SMEM)] * 3
        + [pl.BlockSpec(memory_space=pltpu.VMEM)] * 4,
        out_specs=pl.BlockSpec(memory_space=pltpu.VMEM),
        scratch_shapes=[
            pltpu.VMEM((high.shape[0], substeps, size), F32),
            pltpu.VMEM((blocks, substeps, size), F32),
        ],
        name="pull",
    )(face, owner, node, loads, nodes, high, low)


def local(
    state, previous, coefficient, stiffness, waveform, entry_face, entry_owner, entry_node, rbf
):
    n_sect = lax.axis_size("sect")
    n_dom = lax.axis_size("dom")
    sides, wave, above, below = exchange(state, previous, coefficient, waveform, n_sect, n_dom)
    current, before, trace, outgoing, high, low = window(
        entry_face, entry_owner, entry_node, state, previous, coefficient, stiffness, sides,
        wave, above, below, rbf, n_sect, n_dom,
    )
    loads, nodes = swap(outgoing, trace, n_sect, n_dom)
    out = pull(entry_face, entry_owner, entry_node, loads, nodes, high, low, n_sect, n_dom)
    return (current, before, out)


def solution(mesh):
    in_specs = (
        P("sect", "dom"),
        P("sect", "dom"),
        P("sect", "dom"),
        P(),
        P(None, ("sect", "dom"), None),
        P(("sect", "dom")),
        P(("sect", "dom"), None),
        P(("sect", "dom")),
        P(("sect", "dom"), None, None),
    )
    out_specs = (P("sect", "dom"), P("sect", "dom"), P(None, ("sect", "dom"), None))
    return jax.shard_map(local, mesh=mesh, in_specs=in_specs, out_specs=out_specs, check_vma=False)
```

```python
import functools

import jax
import jax.numpy as jnp
from jax import lax
from jax.experimental import pallas as pl
from jax.experimental.pallas import tpu as pltpu
from jax.sharding import PartitionSpec as P

HALO = 8
TILE = 128
F32 = jnp.float32
BF16 = jnp.bfloat16


def signal(barrier, section, column):
    pl.semaphore_signal(
        barrier, inc=1, device_id=(section, column), device_id_type=pl.DeviceIdType.MESH
    )


def remote(source, target, send, recv, section, column):
    return pltpu.make_async_remote_copy(
        src_ref=source,
        dst_ref=target,
        send_sem=send,
        recv_sem=recv,
        device_id=(section, column),
        device_id_type=pl.DeviceIdType.MESH,
    )


def halo_kernel(n_sect, n_dom, *refs):
    fields = refs[0:3]
    wave_ref = refs[3]
    sides_ref, wave_out, above_ref, below_ref = refs[4:8]
    to_left, to_right, from_left, from_right, to_up, to_down, from_up, from_down = refs[8:16]
    from_up_left, from_up_right, from_down_left, from_down_right = refs[16:20]
    send_sem, recv_sem = refs[20:22]
    s = lax.axis_index("sect")
    d = lax.axis_index("dom")
    rows, lanes = fields[0].shape
    substeps = wave_ref.shape[0]
    has_left = d > 0
    has_right = d < n_dom - 1
    has_up = jnp.logical_and(s >= 1, s <= n_sect - 2)
    has_down = s <= n_sect - 3
    both = jnp.logical_and
    first = pl.ds(0, TILE)
    last = pl.ds(lanes - TILE, TILE)
    routes = (
        (has_up, s - 1, d, to_up, from_down, has_down, from_down),
        (has_down, s + 1, d, to_down, from_up, has_up, from_up),
        (has_left, s, d - 1, to_left, from_right, has_right, from_right),
        (has_right, s, d + 1, to_right, from_left, has_left, from_left),
        (both(has_up, has_left), s - 1, d - 1, to_up.at[:, first], from_down_right,
         both(has_down, has_right), from_down_right),
        (both(has_up, has_right), s - 1, d + 1, to_up.at[:, last], from_down_left,
         both(has_down, has_left), from_down_left),
        (both(has_down, has_left), s + 1, d - 1, to_down.at[:, first], from_up_right,
         both(has_up, has_right), from_up_right),
        (both(has_down, has_right), s + 1, d + 1, to_down.at[:, last], from_up_left,
         both(has_up, has_left), from_up_left),
    )
    barrier = pltpu.get_barrier_semaphore()
    for has, section, column, *_ in routes:

        @pl.when(has)
        def _(section=section, column=column):
            signal(barrier, section, column)

    wave = jnp.concatenate([wave_ref[k] for k in range(substeps)], 0)
    for a in range(3):
        part = pl.ds(a * HALO, HALO)
        to_up[part] = fields[a][:HALO]
        to_down[part] = fields[a][rows - HALO :]
    to_down[3 * HALO :] = wave
    lane = lax.broadcasted_iota(jnp.int32, (rows, TILE), 1)

    def pack(where, start):
        a = fields[0][:, where]
        b = pltpu.roll(fields[1][:, where], (HALO - start) % TILE, 1)
        c = pltpu.roll(fields[2][:, where], (2 * HALO - start) % TILE, 1)
        if start:
            a = pltpu.roll(a, TILE - start, 1)
        packed = jnp.where(lane < HALO, a, jnp.where(lane < 2 * HALO, b, c))
        return packed.T[: 3 * HALO]

    to_left[: 3 * HALO] = pack(first, 0)
    to_left[3 * HALO :, :TILE] = wave[:, :TILE]
    to_left[3 * HALO :, TILE:] = jnp.zeros((HALO, rows - TILE), F32)
    to_right[: 3 * HALO] = pack(last, TILE - HALO)
    to_right[3 * HALO :, :TILE] = wave[:, lanes - TILE :]
    to_right[3 * HALO :, TILE:] = jnp.zeros((HALO, rows - TILE), F32)

    peers = sum(jnp.where(route[0], 1, 0).astype(jnp.int32) for route in routes)
    pl.semaphore_wait(barrier, peers)

    copies = []
    for i, (has, section, column, source, target, _, _) in enumerate(routes):
        copy = remote(source, target, send_sem.at[i], recv_sem.at[i], section, column)
        copies.append(copy)

        @pl.when(has)
        def _(copy=copy):
            copy.start()

    wave_out[:, :lanes] = wave
    for i in (2, 3, 0, 1, 4, 5, 6, 7):
        comes, buf = routes[i][5:]

        @pl.when(comes)
        def _(copy=copies[i]):
            copy.wait_recv()

        @pl.when(jnp.logical_not(comes))
        def _(buf=buf):
            buf[...] = jnp.zeros_like(buf)

        if i == 3:
            fill = jnp.zeros((TILE - 3 * HALO, rows), F32)
            right = jnp.concatenate([from_right[: 3 * HALO], fill], 0).T
            left = jnp.concatenate([from_left[: 3 * HALO], fill], 0).T
            for a in range(3):
                r = pltpu.roll(right, (TILE - a * HALO) % TILE, 1) if a else right
                le = pltpu.roll(left, TILE - (a + 1) * HALO, 1)
                sides_ref[a] = jnp.where(
                    lane < HALO, r, jnp.where(lane >= TILE - HALO, le, 0.0)
                )

    def join(right_part, left_part):
        at = lax.broadcasted_iota(jnp.int32, right_part.shape, 1)
        return jnp.where(at < HALO, right_part, jnp.where(at >= TILE - HALO, left_part, 0.0))

    wave_out[:, lanes:] = join(from_right[3 * HALO :, :TILE], from_left[3 * HALO :, :TILE])
    above_ref[:, :lanes] = from_up[...]
    above_ref[:, lanes:] = join(from_up_right[...], from_up_left[...])
    below_ref[:, :lanes] = from_down[...]
    below_ref[:, lanes:] = join(from_down_right[...], from_down_left[...])

    for route, copy in zip(routes, copies):

        @pl.when(route[0])
        def _(copy=copy):
            copy.wait_send()


def exchange(state, previous, coefficient, wave, n_sect, n_dom):
    rows, lanes = state.shape
    wide = lanes + TILE
    vmem = pl.BlockSpec(memory_space=pltpu.VMEM)
    return pl.pallas_call(
        functools.partial(halo_kernel, n_sect, n_dom),
        out_shape=(
            jax.ShapeDtypeStruct((3, rows, TILE), F32),
            jax.ShapeDtypeStruct((HALO, wide), F32),
            jax.ShapeDtypeStruct((4 * HALO, wide), F32),
            jax.ShapeDtypeStruct((3 * HALO, wide), F32),
        ),
        in_specs=[vmem] * 4,
        out_specs=(vmem,) * 4,
        scratch_shapes=[pltpu.VMEM((4 * HALO, rows), F32)] * 4
        + [
            pltpu.VMEM((3 * HALO, lanes), F32),
            pltpu.VMEM((4 * HALO, lanes), F32),
            pltpu.VMEM((4 * HALO, lanes), F32),
            pltpu.VMEM((3 * HALO, lanes), F32),
            pltpu.VMEM((4 * HALO, TILE), F32),
            pltpu.VMEM((4 * HALO, TILE), F32),
            pltpu.VMEM((3 * HALO, TILE), F32),
            pltpu.VMEM((3 * HALO, TILE), F32),
            pltpu.SemaphoreType.DMA((8,)),
            pltpu.SemaphoreType.DMA((8,)),
        ],
        compiler_params=pltpu.CompilerParams(collective_id=0, has_side_effects=True),
        name="halo",
    )(state, previous, coefficient, wave)


CHUNK = 24


def window_kernel(
    n_sect, face, owner, node, state, previous, coefficient, stiffness, sides, wave, above,
    below, rbf, state_out, previous_out, trace_out, slots, first, second, coef, terms,
    matrices, wave_own, wave_up, weights, sems,
):
    rows, lanes = state.shape
    wide = lanes + TILE
    full = rows + 2 * HALO
    s = lax.axis_index("sect")
    on_shell = s == n_sect - 1
    inner = pl.ds(HALO, rows)
    left = pl.ds(0, lanes)
    moves = [(rbf, weights)]
    for a, (ref, center) in enumerate(((first, state), (second, previous), (coef, coefficient))):
        part = pl.ds(a * HALO, HALO)
        moves += [
            (center, ref.at[inner, left]),
            (sides.at[a], ref.at[inner, pl.ds(lanes, TILE)]),
            (above.at[part], ref.at[pl.ds(0, HALO)]),
            (below.at[part], ref.at[pl.ds(HALO + rows, HALO)]),
        ]
    moves += [
        (wave, wave_own),
        (above.at[pl.ds(3 * HALO, HALO)], wave_up),
        (stiffness, matrices),
    ]
    loads = [
        pltpu.make_async_copy(source, target, sems.at[i])
        for i, (source, target) in enumerate(moves)
    ]
    for copy in loads[1:] + loads[:1]:
        copy.start()
    for copy in loads[1:]:
        copy.wait()
    substeps = wave.shape[0]
    shell_scale = jnp.where(on_shell, 1.0, 0.0).astype(F32)
    fluid_scale = 1.0 - shell_scale
    elem_blocks, elem = stiffness.shape[0], stiffness.shape[1]

    def step(k, cur, other):
        for start in range(0, full, CHUNK):
            stop = min(start + CHUNK, full)
            here = cur[start:stop, :]
            if start == 0:
                up = pltpu.roll(here, 1, 0)
            else:
                up = cur[start - 1 : stop - 1, :]
            if stop == full:
                down = pltpu.roll(here, stop - start - 1, 0)
            else:
                down = cur[start + 1 : stop + 1, :]
            near = (up + down) + pltpu.roll(here, 1, 1) + pltpu.roll(here, wide - 1, 1)
            other[start:stop, :] = (
                2.0 * here - other[start:stop, :] + coef[start:stop, :] * (near - 4.0 * here)
            )
        row = wave_own[pl.ds(k, 1), :]
        up_row = wave_up[pl.ds(k, 1), :]
        other[HALO - 1 : HALO, :] += coef[HALO - 1 : HALO, :] * (up_row * fluid_scale)
        other[HALO : HALO + 1, :] += coef[HALO : HALO + 1, :] * (row * shell_scale)
        at = HALO + rows - 1
        other[at : at + 1, :] += coef[at : at + 1, :] * (row * fluid_scale)

        @pl.when(on_shell)
        def _():
            for b in range(elem_blocks):
                part = slice(HALO + b * elem, HALO + (b + 1) * elem)
                term = jnp.dot(
                    matrices[b], cur[part, :].astype(BF16), preferred_element_type=F32
                )
                other[part, :] -= coef[part, :] * term

        seen = jnp.where(
            on_shell, other[HALO : HALO + 1, :lanes], other[at : at + 1, :lanes]
        )
        for b in range(lanes // TILE):
            trace_out[b, pl.ds(k, 1), :] = seen[:, b * TILE : (b + 1) * TILE]

    def pair(i, carry):
        step(2 * i, first, second)
        step(2 * i + 1, second, first)
        return carry

    lax.fori_loop(0, substeps // 2, pair, 0)
    leave = [
        pltpu.make_async_copy(first.at[inner, left], state_out, sems.at[len(moves)]),
        pltpu.make_async_copy(second.at[inner, left], previous_out, sems.at[len(moves) + 1]),
    ]
    for copy in leave:
        copy.start()
    loads[0].wait()


    entries = rbf.shape[0]
    blocks = trace_out.shape[0]

    @pl.when(jnp.logical_not(on_shell))
    def _():
        slots[...] = jnp.zeros_like(slots)
        for e in range(entries):
            w_high, w_low = split(weights[e])
            terms[e] = three_products(trace_out[face[e]], w_high, w_low, 0)
        for e in range(entries):
            slots[owner[e, 0] * blocks + node[e]] += terms[e]

    for copy in leave:
        copy.wait()


def window(
    face, owner, node, state, previous, coefficient, stiffness, sides, wave, above, below, rbf,
    n_sect, n_dom,
):
    rows, lanes = state.shape
    substeps = wave.shape[0]
    blocks = lanes // TILE
    vmem = pl.BlockSpec(memory_space=pltpu.VMEM)
    return pl.pallas_call(
        functools.partial(window_kernel, n_sect),
        out_shape=(
            jax.ShapeDtypeStruct((rows, lanes), F32),
            jax.ShapeDtypeStruct((rows, lanes), F32),
            jax.ShapeDtypeStruct((blocks, substeps, TILE), F32),
            jax.ShapeDtypeStruct((n_dom * blocks, substeps, TILE), F32),
        ),
        in_specs=[pl.BlockSpec(memory_space=pltpu.SMEM)] * 3
        + [pl.BlockSpec(memory_space=pl.ANY)] * 9,
        out_specs=(pl.BlockSpec(memory_space=pl.ANY),) * 2 + (vmem,) * 2,
        scratch_shapes=[pltpu.VMEM((rows + 2 * HALO, lanes + TILE), F32)] * 3
        + [
            pltpu.VMEM((rbf.shape[0], substeps, TILE), F32),
            pltpu.VMEM(stiffness.shape, BF16),
            pltpu.VMEM(wave.shape, F32),
            pltpu.VMEM(wave.shape, F32),
            pltpu.VMEM(rbf.shape, F32),
            pltpu.SemaphoreType.DMA((18,)),
        ],
        compiler_params=pltpu.CompilerParams(vmem_limit_bytes=16 * 1024 * 1024),
        name="window",
    )(
        face, owner, node, state, previous, coefficient, stiffness, sides, wave, above, below,
        rbf,
    )


def split(value):
    high = value.astype(BF16)
    low = (value - high.astype(F32)).astype(BF16)
    return high, low


def three_products(x, w_high, w_low, contract):
    x_high, x_low = split(x)
    dims = (((1,), (contract,)), ((), ()))
    out = lax.dot_general(x_high, w_high, dims, preferred_element_type=F32)
    out += lax.dot_general(x_low, w_high, dims, preferred_element_type=F32)
    out += lax.dot_general(x_high, w_low, dims, preferred_element_type=F32)
    return out


def swap_kernel(
    n_sect, n_dom, outgoing, trace, loads_out, nodes_out,
    arrived, total, parts, nodes, shell_trace,
    load_send, load_recv, part_send, part_recv, down_send, down_recv, node_send, node_recv,
):
    s = lax.axis_index("sect")
    d = lax.axis_index("dom")
    blocks = trace.shape[0]
    shell = n_sect - 1
    on_shell = s == shell
    barrier = pltpu.get_barrier_semaphore()

    @pl.when(on_shell)
    def _():
        for t in range(shell):
            signal(barrier, t, d)
        pl.semaphore_wait(barrier, shell)

    @pl.when(jnp.logical_not(on_shell))
    def _():
        for j in range(1, n_dom):
            signal(barrier, s, lax.rem(d + j, n_dom))
        signal(barrier, shell, d)
        pl.semaphore_wait(barrier, n_dom)

    @pl.when(on_shell)
    def _():
        copies = []
        for t in range(shell):
            copy = remote(trace, shell_trace, down_send.at[t], down_recv, t, d)
            copy.start()
            copies.append(copy)
        nodes_out[...] = jnp.zeros_like(nodes_out)
        for t in range(shell):
            remote(total, parts.at[t], part_send, part_recv.at[t], t, d).wait_recv()
        loads = parts[0]
        for t in range(1, shell):
            loads = loads + parts[t]
        loads_out[...] = loads
        for copy in copies:
            copy.wait_send()

    @pl.when(jnp.logical_not(on_shell))
    def _():
        loads = []
        for j in range(1, n_dom):
            to = lax.rem(d + j, n_dom)
            copy = remote(
                outgoing.at[pl.ds(to * blocks, blocks)], arrived.at[j - 1],
                load_send.at[j - 1], load_recv.at[j - 1], s, to,
            )
            copy.start()
            loads.append(copy)
        remote(trace, shell_trace, down_send.at[0], down_recv, shell, d).wait_recv()
        sends = []
        for j in range(1, n_dom):
            to = lax.rem(d + j, n_dom)
            copy = remote(
                shell_trace, nodes.at[j - 1], node_send.at[j - 1], node_recv.at[j - 1], s, to
            )
            copy.start()
            sends.append(copy)
        value = outgoing[pl.ds(d * blocks, blocks)]
        for j in range(1, n_dom):
            loads[j - 1].wait_recv()
            value = value + arrived[j - 1]
        total[...] = value
        up = remote(total, parts.at[s], part_send, part_recv.at[s], shell, d)
        up.start()
        loads_out[...] = jnp.zeros_like(loads_out)
        nodes_out[0] = shell_trace[...]
        for j in range(1, n_dom):
            sends[j - 1].wait_recv()
            nodes_out[j] = nodes[j - 1]
        for copy in loads + sends + [up]:
            copy.wait_send()


def swap(outgoing, trace, n_sect, n_dom):
    block = trace.shape
    dma = pltpu.SemaphoreType.DMA
    return pl.pallas_call(
        functools.partial(swap_kernel, n_sect, n_dom),
        out_shape=(
            jax.ShapeDtypeStruct(block, F32),
            jax.ShapeDtypeStruct((n_dom,) + block, F32),
        ),
        in_specs=[pl.BlockSpec(memory_space=pltpu.VMEM)] * 2,
        out_specs=(pl.BlockSpec(memory_space=pltpu.VMEM),) * 2,
        scratch_shapes=[
            pltpu.VMEM((n_dom - 1,) + block, F32),
            pltpu.VMEM(block, F32),
            pltpu.VMEM((n_sect - 1,) + block, F32),
            pltpu.VMEM((n_dom - 1,) + block, F32),
            pltpu.VMEM(block, F32),
            dma((n_dom - 1,)),
            dma((n_dom - 1,)),
            dma,
            dma((n_sect - 1,)),
            dma((n_sect - 1,)),
            dma,
            dma((n_dom - 1,)),
            dma((n_dom - 1,)),
        ],
        compiler_params=pltpu.CompilerParams(collective_id=1, has_side_effects=True),
        name="swap",
    )(outgoing, trace)


def pull_kernel(n_sect, n_dom, face, owner, node, loads, nodes, rbf, out, terms, sums):
    entries = rbf.shape[0]
    substeps = out.shape[0]
    blocks = loads.shape[0]
    d = lax.axis_index("dom")
    on_shell = lax.axis_index("sect") == n_sect - 1

    @pl.when(on_shell)
    def _():
        for b in range(blocks):
            for k in range(substeps):
                out[k, :, b * TILE : (b + 1) * TILE] = loads[b, k : k + 1, :]

    @pl.when(jnp.logical_not(on_shell))
    def _():
        sums[...] = jnp.zeros_like(sums)
        for e in range(entries):
            slot = lax.rem(d - owner[e, 0] + n_dom, n_dom)
            w_high, w_low = split(rbf[e])
            terms[e] = three_products(nodes[slot, node[e]], w_high, w_low, 1)
        for e in range(entries):
            sums[face[e]] += terms[e]
        for b in range(blocks):
            for k in range(substeps):
                out[k, :, b * TILE : (b + 1) * TILE] = sums[b, k : k + 1, :]


def pull(face, owner, node, loads, nodes, rbf, n_sect, n_dom):
    blocks, substeps, size = loads.shape
    return pl.pallas_call(
        functools.partial(pull_kernel, n_sect, n_dom),
        out_shape=jax.ShapeDtypeStruct((substeps, 1, blocks * size), F32),
        in_specs=[pl.BlockSpec(memory_space=pltpu.SMEM)] * 3
        + [pl.BlockSpec(memory_space=pltpu.VMEM)] * 3,
        out_specs=pl.BlockSpec(memory_space=pltpu.VMEM),
        scratch_shapes=[
            pltpu.VMEM((rbf.shape[0], substeps, size), F32),
            pltpu.VMEM((blocks, substeps, size), F32),
        ],
        name="pull",
    )(face, owner, node, loads, nodes, rbf)


def local(
    state, previous, coefficient, stiffness, waveform, entry_face, entry_owner, entry_node, rbf
):
    n_sect = lax.axis_size("sect")
    n_dom = lax.axis_size("dom")
    sides, wave, above, below = exchange(state, previous, coefficient, waveform, n_sect, n_dom)
    current, before, trace, outgoing = window(
        entry_face, entry_owner, entry_node, state, previous, coefficient, stiffness, sides,
        wave, above, below, rbf, n_sect, n_dom,
    )
    loads, nodes = swap(outgoing, trace, n_sect, n_dom)
    out = pull(entry_face, entry_owner, entry_node, loads, nodes, rbf, n_sect, n_dom)
    return (current, before, out)


def solution(mesh):
    in_specs = (
        P("sect", "dom"),
        P("sect", "dom"),
        P("sect", "dom"),
        P(),
        P(None, ("sect", "dom"), None),
        P(("sect", "dom")),
        P(("sect", "dom"), None),
        P(("sect", "dom")),
        P(("sect", "dom"), None, None),
    )
    out_specs = (P("sect", "dom"), P("sect", "dom"), P(None, ("sect", "dom"), None))
    return jax.shard_map(local, mesh=mesh, in_specs=in_specs, out_specs=out_specs, check_vma=False)
```

```python
import functools

import jax
import jax.numpy as jnp
from jax import lax
from jax.experimental import pallas as pl
from jax.experimental.pallas import tpu as pltpu
from jax.sharding import PartitionSpec as P

HALO = 8
TILE = 128
F32 = jnp.float32
BF16 = jnp.bfloat16


def signal(barrier, section, column):
    pl.semaphore_signal(
        barrier, inc=1, device_id=(section, column), device_id_type=pl.DeviceIdType.MESH
    )


def remote(source, target, send, recv, section, column):
    return pltpu.make_async_remote_copy(
        src_ref=source,
        dst_ref=target,
        send_sem=send,
        recv_sem=recv,
        device_id=(section, column),
        device_id_type=pl.DeviceIdType.MESH,
    )


def halo_kernel(n_sect, n_dom, *refs):
    fields = refs[0:3]
    wave_ref = refs[3]
    sides_ref, wave_out, above_ref, below_ref = refs[4:8]
    to_left, to_right, from_left, from_right, to_up, to_down, from_up, from_down = refs[8:16]
    from_up_left, from_up_right, from_down_left, from_down_right = refs[16:20]
    send_sem, recv_sem = refs[20:22]
    s = lax.axis_index("sect")
    d = lax.axis_index("dom")
    rows, lanes = fields[0].shape
    substeps = wave_ref.shape[0]
    has_left = d > 0
    has_right = d < n_dom - 1
    has_up = jnp.logical_and(s >= 1, s <= n_sect - 2)
    has_down = s <= n_sect - 3
    both = jnp.logical_and
    first = pl.ds(0, TILE)
    last = pl.ds(lanes - TILE, TILE)
    routes = (
        (has_up, s - 1, d, to_up, from_down, has_down, from_down),
        (has_down, s + 1, d, to_down, from_up, has_up, from_up),
        (has_left, s, d - 1, to_left, from_right, has_right, from_right),
        (has_right, s, d + 1, to_right, from_left, has_left, from_left),
        (both(has_up, has_left), s - 1, d - 1, to_up.at[:, first], from_down_right,
         both(has_down, has_right), from_down_right),
        (both(has_up, has_right), s - 1, d + 1, to_up.at[:, last], from_down_left,
         both(has_down, has_left), from_down_left),
        (both(has_down, has_left), s + 1, d - 1, to_down.at[:, first], from_up_right,
         both(has_up, has_right), from_up_right),
        (both(has_down, has_right), s + 1, d + 1, to_down.at[:, last], from_up_left,
         both(has_up, has_left), from_up_left),
    )
    barrier = pltpu.get_barrier_semaphore()
    for has, section, column, *_ in routes:

        @pl.when(has)
        def _(section=section, column=column):
            signal(barrier, section, column)

    wave = jnp.concatenate([wave_ref[k] for k in range(substeps)], 0)
    for a in range(3):
        part = pl.ds(a * HALO, HALO)
        to_up[part] = fields[a][:HALO]
        to_down[part] = fields[a][rows - HALO :]
    to_down[3 * HALO :] = wave
    lane = lax.broadcasted_iota(jnp.int32, (rows, TILE), 1)

    def pack(where, start):
        a = fields[0][:, where]
        b = pltpu.roll(fields[1][:, where], (HALO - start) % TILE, 1)
        c = pltpu.roll(fields[2][:, where], (2 * HALO - start) % TILE, 1)
        if start:
            a = pltpu.roll(a, TILE - start, 1)
        packed = jnp.where(lane < HALO, a, jnp.where(lane < 2 * HALO, b, c))
        return packed.T[: 3 * HALO]

    to_left[: 3 * HALO] = pack(first, 0)
    to_left[3 * HALO :, :TILE] = wave[:, :TILE]
    to_left[3 * HALO :, TILE:] = jnp.zeros((HALO, rows - TILE), F32)
    to_right[: 3 * HALO] = pack(last, TILE - HALO)
    to_right[3 * HALO :, :TILE] = wave[:, lanes - TILE :]
    to_right[3 * HALO :, TILE:] = jnp.zeros((HALO, rows - TILE), F32)

    peers = sum(jnp.where(route[0], 1, 0).astype(jnp.int32) for route in routes)
    pl.semaphore_wait(barrier, peers)

    copies = []
    for i, (has, section, column, source, target, _, _) in enumerate(routes):
        copy = remote(source, target, send_sem.at[i], recv_sem.at[i], section, column)
        copies.append(copy)

        @pl.when(has)
        def _(copy=copy):
            copy.start()

    wave_out[:, :lanes] = wave
    for i in (2, 3, 0, 1, 4, 5, 6, 7):
        comes, buf = routes[i][5:]

        @pl.when(comes)
        def _(copy=copies[i]):
            copy.wait_recv()

        @pl.when(jnp.logical_not(comes))
        def _(buf=buf):
            buf[...] = jnp.zeros_like(buf)

        if i == 3:
            fill = jnp.zeros((TILE - 3 * HALO, rows), F32)
            right = jnp.concatenate([from_right[: 3 * HALO], fill], 0).T
            left = jnp.concatenate([from_left[: 3 * HALO], fill], 0).T
            for a in range(3):
                r = pltpu.roll(right, (TILE - a * HALO) % TILE, 1) if a else right
                le = pltpu.roll(left, TILE - (a + 1) * HALO, 1)
                sides_ref[a] = jnp.where(
                    lane < HALO, r, jnp.where(lane >= TILE - HALO, le, 0.0)
                )

    def join(right_part, left_part):
        at = lax.broadcasted_iota(jnp.int32, right_part.shape, 1)
        return jnp.where(at < HALO, right_part, jnp.where(at >= TILE - HALO, left_part, 0.0))

    wave_out[:, lanes:] = join(from_right[3 * HALO :, :TILE], from_left[3 * HALO :, :TILE])
    above_ref[:, :lanes] = from_up[...]
    above_ref[:, lanes:] = join(from_up_right[...], from_up_left[...])
    below_ref[:, :lanes] = from_down[...]
    below_ref[:, lanes:] = join(from_down_right[...], from_down_left[...])

    for route, copy in zip(routes, copies):

        @pl.when(route[0])
        def _(copy=copy):
            copy.wait_send()


def exchange(state, previous, coefficient, wave, n_sect, n_dom):
    rows, lanes = state.shape
    wide = lanes + TILE
    vmem = pl.BlockSpec(memory_space=pltpu.VMEM)
    return pl.pallas_call(
        functools.partial(halo_kernel, n_sect, n_dom),
        out_shape=(
            jax.ShapeDtypeStruct((3, rows, TILE), F32),
            jax.ShapeDtypeStruct((HALO, wide), F32),
            jax.ShapeDtypeStruct((4 * HALO, wide), F32),
            jax.ShapeDtypeStruct((3 * HALO, wide), F32),
        ),
        in_specs=[vmem] * 4,
        out_specs=(vmem,) * 4,
        scratch_shapes=[pltpu.VMEM((4 * HALO, rows), F32)] * 4
        + [
            pltpu.VMEM((3 * HALO, lanes), F32),
            pltpu.VMEM((4 * HALO, lanes), F32),
            pltpu.VMEM((4 * HALO, lanes), F32),
            pltpu.VMEM((3 * HALO, lanes), F32),
            pltpu.VMEM((4 * HALO, TILE), F32),
            pltpu.VMEM((4 * HALO, TILE), F32),
            pltpu.VMEM((3 * HALO, TILE), F32),
            pltpu.VMEM((3 * HALO, TILE), F32),
            pltpu.SemaphoreType.DMA((8,)),
            pltpu.SemaphoreType.DMA((8,)),
        ],
        compiler_params=pltpu.CompilerParams(collective_id=0, has_side_effects=True),
        name="halo",
    )(state, previous, coefficient, wave)


CHUNK = 24


def window_kernel(
    n_sect, face, owner, node, state, previous, coefficient, stiffness, sides, wave, above,
    below, rbf, state_out, previous_out, trace_hbm, slots_hbm, first, second, coef, terms,
    matrices, wave_own, wave_up, weights, trace_out, slots, sems,
):
    rows, lanes = state.shape
    wide = lanes + TILE
    full = rows + 2 * HALO
    s = lax.axis_index("sect")
    on_shell = s == n_sect - 1
    inner = pl.ds(HALO, rows)
    left = pl.ds(0, lanes)
    moves = [(rbf, weights)]
    for a, (ref, center) in enumerate(((first, state), (second, previous), (coef, coefficient))):
        part = pl.ds(a * HALO, HALO)
        moves += [
            (center, ref.at[inner, left]),
            (sides.at[a], ref.at[inner, pl.ds(lanes, TILE)]),
            (above.at[part], ref.at[pl.ds(0, HALO)]),
            (below.at[part], ref.at[pl.ds(HALO + rows, HALO)]),
        ]
    moves += [
        (wave, wave_own),
        (above.at[pl.ds(3 * HALO, HALO)], wave_up),
        (stiffness, matrices),
    ]
    loads = [
        pltpu.make_async_copy(source, target, sems.at[i])
        for i, (source, target) in enumerate(moves)
    ]
    for copy in loads[1:] + loads[:1]:
        copy.start()
    for copy in loads[1:]:
        copy.wait()
    substeps = wave.shape[0]
    shell_scale = jnp.where(on_shell, 1.0, 0.0).astype(F32)
    fluid_scale = 1.0 - shell_scale
    elem_blocks, elem = stiffness.shape[0], stiffness.shape[1]

    def step(k, cur, other):
        for start in range(0, full, CHUNK):
            stop = min(start + CHUNK, full)
            here = cur[start:stop, :]
            if start == 0:
                up = pltpu.roll(here, 1, 0)
            else:
                up = cur[start - 1 : stop - 1, :]
            if stop == full:
                down = pltpu.roll(here, stop - start - 1, 0)
            else:
                down = cur[start + 1 : stop + 1, :]
            near = (up + down) + pltpu.roll(here, 1, 1) + pltpu.roll(here, wide - 1, 1)
            other[start:stop, :] = (
                2.0 * here - other[start:stop, :] + coef[start:stop, :] * (near - 4.0 * here)
            )
        row = wave_own[pl.ds(k, 1), :]
        up_row = wave_up[pl.ds(k, 1), :]
        other[HALO - 1 : HALO, :] += coef[HALO - 1 : HALO, :] * (up_row * fluid_scale)
        other[HALO : HALO + 1, :] += coef[HALO : HALO + 1, :] * (row * shell_scale)
        at = HALO + rows - 1
        other[at : at + 1, :] += coef[at : at + 1, :] * (row * fluid_scale)

        @pl.when(on_shell)
        def _():
            for b in range(elem_blocks):
                part = slice(HALO + b * elem, HALO + (b + 1) * elem)
                term = jnp.dot(
                    matrices[b], cur[part, :].astype(BF16), preferred_element_type=F32
                )
                other[part, :] -= coef[part, :] * term

        seen = jnp.where(
            on_shell, other[HALO : HALO + 1, :lanes], other[at : at + 1, :lanes]
        )
        for b in range(lanes // TILE):
            trace_out[b, pl.ds(k, 1), :] = seen[:, b * TILE : (b + 1) * TILE]

    def pair(i, carry):
        step(2 * i, first, second)
        step(2 * i + 1, second, first)
        return carry

    lax.fori_loop(0, substeps // 2, pair, 0)
    leave = [
        pltpu.make_async_copy(first.at[inner, left], state_out, sems.at[len(moves)]),
        pltpu.make_async_copy(second.at[inner, left], previous_out, sems.at[len(moves) + 1]),
        pltpu.make_async_copy(trace_out, trace_hbm, sems.at[len(moves) + 2]),
    ]
    for copy in leave:
        copy.start()
    loads[0].wait()


    entries = rbf.shape[0]
    blocks = trace_out.shape[0]

    slots[...] = jnp.zeros_like(slots)

    @pl.when(jnp.logical_not(on_shell))
    def _():
        for e in range(entries):
            w_high, w_low = split(weights[e])
            terms[e] = three_products(trace_out[face[e]], w_high, w_low, 0)
        for e in range(entries):
            slots[owner[e, 0] * blocks + node[e]] += terms[e]

    leave.append(pltpu.make_async_copy(slots, slots_hbm, sems.at[len(moves) + 3]))
    leave[-1].start()
    for copy in leave:
        copy.wait()


def window(
    face, owner, node, state, previous, coefficient, stiffness, sides, wave, above, below, rbf,
    n_sect, n_dom,
):
    rows, lanes = state.shape
    substeps = wave.shape[0]
    blocks = lanes // TILE
    return pl.pallas_call(
        functools.partial(window_kernel, n_sect),
        out_shape=(
            jax.ShapeDtypeStruct((rows, lanes), F32),
            jax.ShapeDtypeStruct((rows, lanes), F32),
            jax.ShapeDtypeStruct((blocks, substeps, TILE), F32),
            jax.ShapeDtypeStruct((n_dom * blocks, substeps, TILE), F32),
        ),
        in_specs=[pl.BlockSpec(memory_space=pltpu.SMEM)] * 3
        + [pl.BlockSpec(memory_space=pltpu.HBM)] * 9,
        out_specs=(pl.BlockSpec(memory_space=pltpu.HBM),) * 4,
        scratch_shapes=[pltpu.VMEM((rows + 2 * HALO, lanes + TILE), F32)] * 3
        + [
            pltpu.VMEM((rbf.shape[0], substeps, TILE), F32),
            pltpu.VMEM(stiffness.shape, BF16),
            pltpu.VMEM(wave.shape, F32),
            pltpu.VMEM(wave.shape, F32),
            pltpu.VMEM(rbf.shape, F32),
            pltpu.VMEM((blocks, substeps, TILE), F32),
            pltpu.VMEM((n_dom * blocks, substeps, TILE), F32),
            pltpu.SemaphoreType.DMA((20,)),
        ],
        compiler_params=pltpu.CompilerParams(vmem_limit_bytes=60 * 1024 * 1024),
        name="window",
    )(
        face, owner, node, state, previous, coefficient, stiffness, sides, wave, above, below,
        rbf,
    )


def split(value):
    high = value.astype(BF16)
    low = (value - high.astype(F32)).astype(BF16)
    return high, low


def three_products(x, w_high, w_low, contract):
    x_high, x_low = split(x)
    dims = (((1,), (contract,)), ((), ()))
    out = lax.dot_general(x_high, w_high, dims, preferred_element_type=F32)
    out += lax.dot_general(x_low, w_high, dims, preferred_element_type=F32)
    out += lax.dot_general(x_high, w_low, dims, preferred_element_type=F32)
    return out


def swap_kernel(
    n_sect, n_dom, outgoing, trace, loads_out, nodes_out,
    arrived, total, parts, nodes, shell_trace,
    load_send, load_recv, part_send, part_recv, down_send, down_recv, node_send, node_recv,
):
    s = lax.axis_index("sect")
    d = lax.axis_index("dom")
    blocks = trace.shape[0]
    shell = n_sect - 1
    on_shell = s == shell
    barrier = pltpu.get_barrier_semaphore()

    @pl.when(on_shell)
    def _():
        for t in range(shell):
            signal(barrier, t, d)
        pl.semaphore_wait(barrier, shell)

    @pl.when(jnp.logical_not(on_shell))
    def _():
        for j in range(1, n_dom):
            signal(barrier, s, lax.rem(d + j, n_dom))
        signal(barrier, shell, d)
        pl.semaphore_wait(barrier, n_dom)

    @pl.when(on_shell)
    def _():
        copies = []
        for t in range(shell):
            copy = remote(trace, shell_trace, down_send.at[t], down_recv, t, d)
            copy.start()
            copies.append(copy)
        nodes_out[...] = jnp.zeros_like(nodes_out)
        for t in range(shell):
            remote(total, parts.at[t], part_send, part_recv.at[t], t, d).wait_recv()
        loads = parts[0]
        for t in range(1, shell):
            loads = loads + parts[t]
        loads_out[...] = loads
        for copy in copies:
            copy.wait_send()

    @pl.when(jnp.logical_not(on_shell))
    def _():
        loads = []
        for j in range(1, n_dom):
            to = lax.rem(d + j, n_dom)
            copy = remote(
                outgoing.at[pl.ds(to * blocks, blocks)], arrived.at[j - 1],
                load_send.at[j - 1], load_recv.at[j - 1], s, to,
            )
            copy.start()
            loads.append(copy)
        remote(trace, shell_trace, down_send.at[0], down_recv, shell, d).wait_recv()
        sends = []
        for j in range(1, n_dom):
            to = lax.rem(d + j, n_dom)
            copy = remote(
                shell_trace, nodes.at[j - 1], node_send.at[j - 1], node_recv.at[j - 1], s, to
            )
            copy.start()
            sends.append(copy)
        value = outgoing[pl.ds(d * blocks, blocks)]
        for j in range(1, n_dom):
            loads[j - 1].wait_recv()
            value = value + arrived[j - 1]
        total[...] = value
        up = remote(total, parts.at[s], part_send, part_recv.at[s], shell, d)
        up.start()
        loads_out[...] = jnp.zeros_like(loads_out)
        nodes_out[0] = shell_trace[...]
        for j in range(1, n_dom):
            sends[j - 1].wait_recv()
            nodes_out[j] = nodes[j - 1]
        for copy in loads + sends + [up]:
            copy.wait_send()


def swap(outgoing, trace, n_sect, n_dom):
    block = trace.shape
    dma = pltpu.SemaphoreType.DMA
    return pl.pallas_call(
        functools.partial(swap_kernel, n_sect, n_dom),
        out_shape=(
            jax.ShapeDtypeStruct(block, F32),
            jax.ShapeDtypeStruct((n_dom,) + block, F32),
        ),
        in_specs=[pl.BlockSpec(memory_space=pltpu.VMEM)] * 2,
        out_specs=(pl.BlockSpec(memory_space=pltpu.VMEM),) * 2,
        scratch_shapes=[
            pltpu.VMEM((n_dom - 1,) + block, F32),
            pltpu.VMEM(block, F32),
            pltpu.VMEM((n_sect - 1,) + block, F32),
            pltpu.VMEM((n_dom - 1,) + block, F32),
            pltpu.VMEM(block, F32),
            dma((n_dom - 1,)),
            dma((n_dom - 1,)),
            dma,
            dma((n_sect - 1,)),
            dma((n_sect - 1,)),
            dma,
            dma((n_dom - 1,)),
            dma((n_dom - 1,)),
        ],
        compiler_params=pltpu.CompilerParams(collective_id=1, has_side_effects=True),
        name="swap",
    )(outgoing, trace)


def pull_kernel(n_sect, n_dom, face, owner, node, loads, nodes, rbf, out, terms, sums):
    entries = rbf.shape[0]
    substeps = out.shape[0]
    blocks = loads.shape[0]
    d = lax.axis_index("dom")
    on_shell = lax.axis_index("sect") == n_sect - 1

    @pl.when(on_shell)
    def _():
        for b in range(blocks):
            for k in range(substeps):
                out[k, :, b * TILE : (b + 1) * TILE] = loads[b, k : k + 1, :]

    @pl.when(jnp.logical_not(on_shell))
    def _():
        sums[...] = jnp.zeros_like(sums)
        for e in range(entries):
            slot = lax.rem(d - owner[e, 0] + n_dom, n_dom)
            w_high, w_low = split(rbf[e])
            terms[e] = three_products(nodes[slot, node[e]], w_high, w_low, 1)
        for e in range(entries):
            sums[face[e]] += terms[e]
        for b in range(blocks):
            for k in range(substeps):
                out[k, :, b * TILE : (b + 1) * TILE] = sums[b, k : k + 1, :]


def pull(face, owner, node, loads, nodes, rbf, n_sect, n_dom):
    blocks, substeps, size = loads.shape
    return pl.pallas_call(
        functools.partial(pull_kernel, n_sect, n_dom),
        out_shape=jax.ShapeDtypeStruct((substeps, 1, blocks * size), F32),
        in_specs=[pl.BlockSpec(memory_space=pltpu.SMEM)] * 3
        + [pl.BlockSpec(memory_space=pltpu.VMEM)] * 3,
        out_specs=pl.BlockSpec(memory_space=pltpu.VMEM),
        scratch_shapes=[
            pltpu.VMEM((rbf.shape[0], substeps, size), F32),
            pltpu.VMEM((blocks, substeps, size), F32),
        ],
        name="pull",
    )(face, owner, node, loads, nodes, rbf)


def local(
    state, previous, coefficient, stiffness, waveform, entry_face, entry_owner, entry_node, rbf
):
    n_sect = lax.axis_size("sect")
    n_dom = lax.axis_size("dom")
    sides, wave, above, below = exchange(state, previous, coefficient, waveform, n_sect, n_dom)
    current, before, trace, outgoing = window(
        entry_face, entry_owner, entry_node, state, previous, coefficient, stiffness, sides,
        wave, above, below, rbf, n_sect, n_dom,
    )
    loads, nodes = swap(outgoing, trace, n_sect, n_dom)
    out = pull(entry_face, entry_owner, entry_node, loads, nodes, rbf, n_sect, n_dom)
    return (current, before, out)


def solution(mesh):
    in_specs = (
        P("sect", "dom"),
        P("sect", "dom"),
        P("sect", "dom"),
        P(),
        P(None, ("sect", "dom"), None),
        P(("sect", "dom")),
        P(("sect", "dom"), None),
        P(("sect", "dom")),
        P(("sect", "dom"), None, None),
    )
    out_specs = (P("sect", "dom"), P("sect", "dom"), P(None, ("sect", "dom"), None))
    return jax.shard_map(local, mesh=mesh, in_specs=in_specs, out_specs=out_specs, check_vma=False)
```

```python
import functools

import jax
import jax.numpy as jnp
from jax import lax
from jax.experimental import pallas as pl
from jax.experimental.pallas import tpu as pltpu
from jax.sharding import PartitionSpec as P

HALO = 8
TILE = 128
F32 = jnp.float32
BF16 = jnp.bfloat16


def signal(barrier, section, column):
    pl.semaphore_signal(
        barrier, inc=1, device_id=(section, column), device_id_type=pl.DeviceIdType.MESH
    )


def remote(source, target, send, recv, section, column):
    return pltpu.make_async_remote_copy(
        src_ref=source,
        dst_ref=target,
        send_sem=send,
        recv_sem=recv,
        device_id=(section, column),
        device_id_type=pl.DeviceIdType.MESH,
    )


def halo_kernel(n_sect, n_dom, *refs):
    fields = refs[0:3]
    wave_ref = refs[3]
    sides_ref, wave_out, above_ref, below_ref = refs[4:8]
    to_left, to_right, from_left, from_right, to_up, to_down, from_up, from_down = refs[8:16]
    from_up_left, from_up_right, from_down_left, from_down_right = refs[16:20]
    send_sem, recv_sem, tiles, edge_sem = refs[20:24]
    s = lax.axis_index("sect")
    d = lax.axis_index("dom")
    rows, lanes = fields[0].shape
    substeps = wave_ref.shape[0]
    has_left = d > 0
    has_right = d < n_dom - 1
    has_up = jnp.logical_and(s >= 1, s <= n_sect - 2)
    has_down = s <= n_sect - 3
    both = jnp.logical_and
    first = pl.ds(0, TILE)
    last = pl.ds(lanes - TILE, TILE)
    routes = (
        (has_up, s - 1, d, to_up, from_down, has_down, from_down),
        (has_down, s + 1, d, to_down, from_up, has_up, from_up),
        (has_left, s, d - 1, to_left, from_right, has_right, from_right),
        (has_right, s, d + 1, to_right, from_left, has_left, from_left),
        (both(has_up, has_left), s - 1, d - 1, to_up.at[:, first], from_down_right,
         both(has_down, has_right), from_down_right),
        (both(has_up, has_right), s - 1, d + 1, to_up.at[:, last], from_down_left,
         both(has_down, has_left), from_down_left),
        (both(has_down, has_left), s + 1, d - 1, to_down.at[:, first], from_up_right,
         both(has_up, has_right), from_up_right),
        (both(has_down, has_right), s + 1, d + 1, to_down.at[:, last], from_up_left,
         both(has_up, has_left), from_up_left),
    )
    barrier = pltpu.get_barrier_semaphore()
    for has, section, column, *_ in routes:

        @pl.when(has)
        def _(section=section, column=column):
            signal(barrier, section, column)

    wave = jnp.concatenate([wave_ref[k] for k in range(substeps)], 0)
    edges = []
    for a in range(3):
        part = pl.ds(a * HALO, HALO)
        for source, target in (
            (fields[a].at[:, first], tiles.at[0, a]),
            (fields[a].at[:, last], tiles.at[1, a]),
            (fields[a].at[pl.ds(0, HALO)], to_up.at[part]),
            (fields[a].at[pl.ds(rows - HALO, HALO)], to_down.at[part]),
        ):
            copy = pltpu.make_async_copy(source, target, edge_sem.at[len(edges)])
            copy.start()
            edges.append(copy)
    to_down[3 * HALO :] = wave
    for copy in edges:
        copy.wait()
    lane = lax.broadcasted_iota(jnp.int32, (rows, TILE), 1)

    def pack(where, start):
        a = tiles[where, 0]
        b = pltpu.roll(tiles[where, 1], (HALO - start) % TILE, 1)
        c = pltpu.roll(tiles[where, 2], (2 * HALO - start) % TILE, 1)
        if start:
            a = pltpu.roll(a, TILE - start, 1)
        packed = jnp.where(lane < HALO, a, jnp.where(lane < 2 * HALO, b, c))
        return packed.T[: 3 * HALO]

    to_left[: 3 * HALO] = pack(0, 0)
    to_left[3 * HALO :, :TILE] = wave[:, :TILE]
    to_left[3 * HALO :, TILE:] = jnp.zeros((HALO, rows - TILE), F32)
    to_right[: 3 * HALO] = pack(1, TILE - HALO)
    to_right[3 * HALO :, :TILE] = wave[:, lanes - TILE :]
    to_right[3 * HALO :, TILE:] = jnp.zeros((HALO, rows - TILE), F32)

    peers = sum(jnp.where(route[0], 1, 0).astype(jnp.int32) for route in routes)
    pl.semaphore_wait(barrier, peers)

    copies = []
    for i, (has, section, column, source, target, _, _) in enumerate(routes):
        copy = remote(source, target, send_sem.at[i], recv_sem.at[i], section, column)
        copies.append(copy)

        @pl.when(has)
        def _(copy=copy):
            copy.start()

    wave_out[:, :lanes] = wave
    for i in (2, 3, 0, 1, 4, 5, 6, 7):
        comes, buf = routes[i][5:]

        @pl.when(comes)
        def _(copy=copies[i]):
            copy.wait_recv()

        @pl.when(jnp.logical_not(comes))
        def _(buf=buf):
            buf[...] = jnp.zeros_like(buf)

        if i == 3:
            fill = jnp.zeros((TILE - 3 * HALO, rows), F32)
            right = jnp.concatenate([from_right[: 3 * HALO], fill], 0).T
            left = jnp.concatenate([from_left[: 3 * HALO], fill], 0).T
            for a in range(3):
                r = pltpu.roll(right, (TILE - a * HALO) % TILE, 1) if a else right
                le = pltpu.roll(left, TILE - (a + 1) * HALO, 1)
                sides_ref[a] = jnp.where(
                    lane < HALO, r, jnp.where(lane >= TILE - HALO, le, 0.0)
                )

    def join(right_part, left_part):
        at = lax.broadcasted_iota(jnp.int32, right_part.shape, 1)
        return jnp.where(at < HALO, right_part, jnp.where(at >= TILE - HALO, left_part, 0.0))

    wave_out[:, lanes:] = join(from_right[3 * HALO :, :TILE], from_left[3 * HALO :, :TILE])
    above_ref[:, :lanes] = from_up[...]
    above_ref[:, lanes:] = join(from_up_right[...], from_up_left[...])
    below_ref[:, :lanes] = from_down[...]
    below_ref[:, lanes:] = join(from_down_right[...], from_down_left[...])

    for route, copy in zip(routes, copies):

        @pl.when(route[0])
        def _(copy=copy):
            copy.wait_send()


def exchange(state, previous, coefficient, wave, n_sect, n_dom):
    rows, lanes = state.shape
    wide = lanes + TILE
    vmem = pl.BlockSpec(memory_space=pltpu.VMEM)
    return pl.pallas_call(
        functools.partial(halo_kernel, n_sect, n_dom),
        out_shape=(
            jax.ShapeDtypeStruct((3, rows, TILE), F32),
            jax.ShapeDtypeStruct((HALO, wide), F32),
            jax.ShapeDtypeStruct((4 * HALO, wide), F32),
            jax.ShapeDtypeStruct((3 * HALO, wide), F32),
        ),
        in_specs=[pl.BlockSpec(memory_space=pl.ANY)] * 3 + [vmem],
        out_specs=(vmem,) * 4,
        scratch_shapes=[pltpu.VMEM((4 * HALO, rows), F32)] * 4
        + [
            pltpu.VMEM((3 * HALO, lanes), F32),
            pltpu.VMEM((4 * HALO, lanes), F32),
            pltpu.VMEM((4 * HALO, lanes), F32),
            pltpu.VMEM((3 * HALO, lanes), F32),
            pltpu.VMEM((4 * HALO, TILE), F32),
            pltpu.VMEM((4 * HALO, TILE), F32),
            pltpu.VMEM((3 * HALO, TILE), F32),
            pltpu.VMEM((3 * HALO, TILE), F32),
            pltpu.SemaphoreType.DMA((8,)),
            pltpu.SemaphoreType.DMA((8,)),
            pltpu.VMEM((2, 3, rows, TILE), F32),
            pltpu.SemaphoreType.DMA((12,)),
        ],
        compiler_params=pltpu.CompilerParams(
            collective_id=0, has_side_effects=True, vmem_limit_bytes=60 * 1024 * 1024
        ),
        name="halo",
    )(state, previous, coefficient, wave)


CHUNK = 24


def window_kernel(
    n_sect, face, owner, node, state, previous, coefficient, stiffness, sides, wave, above,
    below, rbf, state_out, previous_out, trace_hbm, slots_hbm, first, second, coef, terms,
    matrices, wave_own, wave_up, weights, trace_out, slots, sems,
):
    rows, lanes = state.shape
    wide = lanes + TILE
    full = rows + 2 * HALO
    s = lax.axis_index("sect")
    on_shell = s == n_sect - 1
    inner = pl.ds(HALO, rows)
    left = pl.ds(0, lanes)
    moves = [(rbf, weights)]
    for a, (ref, center) in enumerate(((first, state), (second, previous), (coef, coefficient))):
        part = pl.ds(a * HALO, HALO)
        moves += [
            (center, ref.at[inner, left]),
            (sides.at[a], ref.at[inner, pl.ds(lanes, TILE)]),
            (above.at[part], ref.at[pl.ds(0, HALO)]),
            (below.at[part], ref.at[pl.ds(HALO + rows, HALO)]),
        ]
    moves += [
        (wave, wave_own),
        (above.at[pl.ds(3 * HALO, HALO)], wave_up),
        (stiffness, matrices),
    ]
    loads = [
        pltpu.make_async_copy(source, target, sems.at[i])
        for i, (source, target) in enumerate(moves)
    ]
    for copy in loads[1:] + loads[:1]:
        copy.start()
    for copy in loads[1:]:
        copy.wait()
    substeps = wave.shape[0]
    shell_scale = jnp.where(on_shell, 1.0, 0.0).astype(F32)
    fluid_scale = 1.0 - shell_scale
    elem_blocks, elem = stiffness.shape[0], stiffness.shape[1]

    def step(k, cur, other):
        for start in range(0, full, CHUNK):
            stop = min(start + CHUNK, full)
            here = cur[start:stop, :]
            if start == 0:
                up = pltpu.roll(here, 1, 0)
            else:
                up = cur[start - 1 : stop - 1, :]
            if stop == full:
                down = pltpu.roll(here, stop - start - 1, 0)
            else:
                down = cur[start + 1 : stop + 1, :]
            near = (up + down) + pltpu.roll(here, 1, 1) + pltpu.roll(here, wide - 1, 1)
            other[start:stop, :] = (
                2.0 * here - other[start:stop, :] + coef[start:stop, :] * (near - 4.0 * here)
            )
        row = wave_own[pl.ds(k, 1), :]
        up_row = wave_up[pl.ds(k, 1), :]
        other[HALO - 1 : HALO, :] += coef[HALO - 1 : HALO, :] * (up_row * fluid_scale)
        other[HALO : HALO + 1, :] += coef[HALO : HALO + 1, :] * (row * shell_scale)
        at = HALO + rows - 1
        other[at : at + 1, :] += coef[at : at + 1, :] * (row * fluid_scale)

        @pl.when(on_shell)
        def _():
            for b in range(elem_blocks):
                part = slice(HALO + b * elem, HALO + (b + 1) * elem)
                term = jnp.dot(
                    matrices[b], cur[part, :].astype(BF16), preferred_element_type=F32
                )
                other[part, :] -= coef[part, :] * term

        seen = jnp.where(
            on_shell, other[HALO : HALO + 1, :lanes], other[at : at + 1, :lanes]
        )
        for b in range(lanes // TILE):
            trace_out[b, pl.ds(k, 1), :] = seen[:, b * TILE : (b + 1) * TILE]

    def pair(i, carry):
        step(2 * i, first, second)
        step(2 * i + 1, second, first)
        return carry

    lax.fori_loop(0, substeps // 2, pair, 0)
    leave = [
        pltpu.make_async_copy(first.at[inner, left], state_out, sems.at[len(moves)]),
        pltpu.make_async_copy(second.at[inner, left], previous_out, sems.at[len(moves) + 1]),
        pltpu.make_async_copy(trace_out, trace_hbm, sems.at[len(moves) + 2]),
    ]
    for copy in leave:
        copy.start()
    loads[0].wait()


    entries = rbf.shape[0]
    blocks = trace_out.shape[0]

    slots[...] = jnp.zeros_like(slots)

    @pl.when(jnp.logical_not(on_shell))
    def _():
        for e in range(entries):
            w_high, w_low = split(weights[e])
            terms[e] = three_products(trace_out[face[e]], w_high, w_low, 0)
        for e in range(entries):
            slots[owner[e, 0] * blocks + node[e]] += terms[e]

    leave.append(pltpu.make_async_copy(slots, slots_hbm, sems.at[len(moves) + 3]))
    leave[-1].start()
    for copy in leave:
        copy.wait()


def window(
    face, owner, node, state, previous, coefficient, stiffness, sides, wave, above, below, rbf,
    n_sect, n_dom,
):
    rows, lanes = state.shape
    substeps = wave.shape[0]
    blocks = lanes // TILE
    return pl.pallas_call(
        functools.partial(window_kernel, n_sect),
        out_shape=(
            jax.ShapeDtypeStruct((rows, lanes), F32),
            jax.ShapeDtypeStruct((rows, lanes), F32),
            jax.ShapeDtypeStruct((blocks, substeps, TILE), F32),
            jax.ShapeDtypeStruct((n_dom * blocks, substeps, TILE), F32),
        ),
        in_specs=[pl.BlockSpec(memory_space=pltpu.SMEM)] * 3
        + [pl.BlockSpec(memory_space=pltpu.HBM)] * 9,
        out_specs=(pl.BlockSpec(memory_space=pltpu.HBM),) * 4,
        scratch_shapes=[pltpu.VMEM((rows + 2 * HALO, lanes + TILE), F32)] * 3
        + [
            pltpu.VMEM((rbf.shape[0], substeps, TILE), F32),
            pltpu.VMEM(stiffness.shape, BF16),
            pltpu.VMEM(wave.shape, F32),
            pltpu.VMEM(wave.shape, F32),
            pltpu.VMEM(rbf.shape, F32),
            pltpu.VMEM((blocks, substeps, TILE), F32),
            pltpu.VMEM((n_dom * blocks, substeps, TILE), F32),
            pltpu.SemaphoreType.DMA((20,)),
        ],
        compiler_params=pltpu.CompilerParams(vmem_limit_bytes=60 * 1024 * 1024),
        name="window",
    )(
        face, owner, node, state, previous, coefficient, stiffness, sides, wave, above, below,
        rbf,
    )


def split(value):
    high = value.astype(BF16)
    low = (value - high.astype(F32)).astype(BF16)
    return high, low


def three_products(x, w_high, w_low, contract):
    x_high, x_low = split(x)
    dims = (((1,), (contract,)), ((), ()))
    out = lax.dot_general(x_high, w_high, dims, preferred_element_type=F32)
    out += lax.dot_general(x_low, w_high, dims, preferred_element_type=F32)
    out += lax.dot_general(x_high, w_low, dims, preferred_element_type=F32)
    return out


def swap_kernel(
    n_sect, n_dom, outgoing, trace, loads_out, nodes_out,
    arrived, total, parts, nodes, shell_trace,
    load_send, load_recv, part_send, part_recv, down_send, down_recv, node_send, node_recv,
):
    s = lax.axis_index("sect")
    d = lax.axis_index("dom")
    blocks = trace.shape[0]
    shell = n_sect - 1
    on_shell = s == shell
    barrier = pltpu.get_barrier_semaphore()

    @pl.when(on_shell)
    def _():
        for t in range(shell):
            signal(barrier, t, d)
        pl.semaphore_wait(barrier, shell)

    @pl.when(jnp.logical_not(on_shell))
    def _():
        for j in range(1, n_dom):
            signal(barrier, s, lax.rem(d + j, n_dom))
        signal(barrier, shell, d)
        pl.semaphore_wait(barrier, n_dom)

    @pl.when(on_shell)
    def _():
        copies = []
        for t in range(shell):
            copy = remote(trace, shell_trace, down_send.at[t], down_recv, t, d)
            copy.start()
            copies.append(copy)
        nodes_out[...] = jnp.zeros_like(nodes_out)
        for t in range(shell):
            remote(total, parts.at[t], part_send, part_recv.at[t], t, d).wait_recv()
        loads = parts[0]
        for t in range(1, shell):
            loads = loads + parts[t]
        loads_out[...] = loads
        for copy in copies:
            copy.wait_send()

    @pl.when(jnp.logical_not(on_shell))
    def _():
        loads = []
        for j in range(1, n_dom):
            to = lax.rem(d + j, n_dom)
            copy = remote(
                outgoing.at[pl.ds(to * blocks, blocks)], arrived.at[j - 1],
                load_send.at[j - 1], load_recv.at[j - 1], s, to,
            )
            copy.start()
            loads.append(copy)
        remote(trace, shell_trace, down_send.at[0], down_recv, shell, d).wait_recv()
        sends = []
        for j in range(1, n_dom):
            to = lax.rem(d + j, n_dom)
            copy = remote(
                shell_trace, nodes.at[j - 1], node_send.at[j - 1], node_recv.at[j - 1], s, to
            )
            copy.start()
            sends.append(copy)
        value = outgoing[pl.ds(d * blocks, blocks)]
        for j in range(1, n_dom):
            loads[j - 1].wait_recv()
            value = value + arrived[j - 1]
        total[...] = value
        up = remote(total, parts.at[s], part_send, part_recv.at[s], shell, d)
        up.start()
        loads_out[...] = jnp.zeros_like(loads_out)
        nodes_out[0] = shell_trace[...]
        for j in range(1, n_dom):
            sends[j - 1].wait_recv()
            nodes_out[j] = nodes[j - 1]
        for copy in loads + sends + [up]:
            copy.wait_send()


def swap(outgoing, trace, n_sect, n_dom):
    block = trace.shape
    dma = pltpu.SemaphoreType.DMA
    return pl.pallas_call(
        functools.partial(swap_kernel, n_sect, n_dom),
        out_shape=(
            jax.ShapeDtypeStruct(block, F32),
            jax.ShapeDtypeStruct((n_dom,) + block, F32),
        ),
        in_specs=[pl.BlockSpec(memory_space=pltpu.VMEM)] * 2,
        out_specs=(pl.BlockSpec(memory_space=pltpu.VMEM),) * 2,
        scratch_shapes=[
            pltpu.VMEM((n_dom - 1,) + block, F32),
            pltpu.VMEM(block, F32),
            pltpu.VMEM((n_sect - 1,) + block, F32),
            pltpu.VMEM((n_dom - 1,) + block, F32),
            pltpu.VMEM(block, F32),
            dma((n_dom - 1,)),
            dma((n_dom - 1,)),
            dma,
            dma((n_sect - 1,)),
            dma((n_sect - 1,)),
            dma,
            dma((n_dom - 1,)),
            dma((n_dom - 1,)),
        ],
        compiler_params=pltpu.CompilerParams(collective_id=1, has_side_effects=True),
        name="swap",
    )(outgoing, trace)


def pull_kernel(n_sect, n_dom, face, owner, node, loads, nodes, rbf, out, terms, sums):
    entries = rbf.shape[0]
    substeps = out.shape[0]
    blocks = loads.shape[0]
    d = lax.axis_index("dom")
    on_shell = lax.axis_index("sect") == n_sect - 1

    @pl.when(on_shell)
    def _():
        for b in range(blocks):
            for k in range(substeps):
                out[k, :, b * TILE : (b + 1) * TILE] = loads[b, k : k + 1, :]

    @pl.when(jnp.logical_not(on_shell))
    def _():
        sums[...] = jnp.zeros_like(sums)
        for e in range(entries):
            slot = lax.rem(d - owner[e, 0] + n_dom, n_dom)
            w_high, w_low = split(rbf[e])
            terms[e] = three_products(nodes[slot, node[e]], w_high, w_low, 1)
        for e in range(entries):
            sums[face[e]] += terms[e]
        for b in range(blocks):
            for k in range(substeps):
                out[k, :, b * TILE : (b + 1) * TILE] = sums[b, k : k + 1, :]


def pull(face, owner, node, loads, nodes, rbf, n_sect, n_dom):
    blocks, substeps, size = loads.shape
    return pl.pallas_call(
        functools.partial(pull_kernel, n_sect, n_dom),
        out_shape=jax.ShapeDtypeStruct((substeps, 1, blocks * size), F32),
        in_specs=[pl.BlockSpec(memory_space=pltpu.SMEM)] * 3
        + [pl.BlockSpec(memory_space=pltpu.VMEM)] * 3,
        out_specs=pl.BlockSpec(memory_space=pltpu.VMEM),
        scratch_shapes=[
            pltpu.VMEM((rbf.shape[0], substeps, size), F32),
            pltpu.VMEM((blocks, substeps, size), F32),
        ],
        name="pull",
    )(face, owner, node, loads, nodes, rbf)


def local(
    state, previous, coefficient, stiffness, waveform, entry_face, entry_owner, entry_node, rbf
):
    n_sect = lax.axis_size("sect")
    n_dom = lax.axis_size("dom")
    sides, wave, above, below = exchange(state, previous, coefficient, waveform, n_sect, n_dom)
    current, before, trace, outgoing = window(
        entry_face, entry_owner, entry_node, state, previous, coefficient, stiffness, sides,
        wave, above, below, rbf, n_sect, n_dom,
    )
    loads, nodes = swap(outgoing, trace, n_sect, n_dom)
    out = pull(entry_face, entry_owner, entry_node, loads, nodes, rbf, n_sect, n_dom)
    return (current, before, out)


def solution(mesh):
    in_specs = (
        P("sect", "dom"),
        P("sect", "dom"),
        P("sect", "dom"),
        P(),
        P(None, ("sect", "dom"), None),
        P(("sect", "dom")),
        P(("sect", "dom"), None),
        P(("sect", "dom")),
        P(("sect", "dom"), None, None),
    )
    out_specs = (P("sect", "dom"), P("sect", "dom"), P(None, ("sect", "dom"), None))
    return jax.shard_map(local, mesh=mesh, in_specs=in_specs, out_specs=out_specs, check_vma=False)
```
